512 devices in a mesh: rows: 128 (over z, y, core), edges: 4 (over x).
Axes of the slice: x: 4, y: 4, z: 16, core: 2. Of those that a mesh axis runs over, the one named last changes fastest.
Arguments:
- features: bfloat16 [655360, 256], P(('rows', 'edges')), may hold values from -6 to 6
- edge_src: int32 [655360], P(('rows', 'edges')), may hold values from 0 to 16383, as said below
- edge_dst: int32 [655360], P(('rows', 'edges')), may hold values from 0 to 16383, as said below
- edge_cell: int32 [655360], P(('rows', 'edges')), may hold values from 0 to 2
- cell_bias: bfloat16 [3, 512], replicated, may hold values from -4 to 4
- w_in: bfloat16 [256, 512], replicated, may hold values from -0.375 to 0.375
- w_out: bfloat16 [256, 256], replicated, may hold values from -0.0068359375 to 0.0068359375
- vectors: float32 [128, 262144], P('edges', 'rows'), may hold values from -6 to 6
- cheb_coef: float32 [5], replicated, may hold values from 0.5 to 1.5
Outputs:
- filtered: float32 [128, 262144], P('edges', 'rows')
The draws below stay inside these ranges and needn't reach their ends.
Inputs may be any that keep to these rules, and one draw needn't show every extreme that they name: `edge_src`: number the devices d = 0 .. 16384 / 32 - 1 along rows and edges together (rows first) and let quarter q be atoms q * 32 to (q + 1) * 32 - 1. Device d holds 1280 edges in order of source atom (cyclically): first the edges of quarter d - 1 it holds, then edges of quarter d, then edges of quarter d + 1 (cyclically over devices). Between 160 and 320 belong to quarter d - 1 and between 160 and 320 to quarter d + 1; for each kind, some device has exactly 320. `edge_dst`: each source, target pair occurs once. The target's tile (atom // 8) lies within 3 tiles of the source's tile, cyclically over 16384 / 8 tiles.
All inputs are finite; a program needn't handle non-finite values.
Results may differ from the reference program's by a relative error of at most 0.0065.
Values may be sent and summed in bfloat16 or wider, within the bound.
A program may use at most 64 MiB of HBM per device.

```python
import jax
import jax.numpy as jnp
from jax import lax

ORB = 16
TILE_ATOMS = 8
BAND = 3
NEIGH = 40
FEAT = 256
HID = 256
VEC = 128
STEPS = 4
ATOM_Q = 32
E_DEV = 1280
SPILL = 320
NATOM = 16384
EDGES = 655360
NROWS = 262144


def edge_lists(key):
    nquart = NATOM // ATOM_Q
    ntiles = NATOM // TILE_ATOMS
    ncand = (2 * BAND + 1) * TILE_ATOMS
    keys = jax.random.split(jax.random.fold_in(key, 11), 7)
    half = SPILL // 2
    low = half + jax.random.randint(keys[0], (nquart,), 0, half + 1)
    high = half + jax.random.randint(keys[1], (nquart,), 0, half + 1)
    low = low.at[jax.random.randint(keys[2], (), 0, nquart)].set(SPILL)
    high = high.at[jax.random.randint(keys[3], (), 0, nquart)].set(SPILL)
    own = E_DEV - low - high
    qsize = own + jnp.roll(high, 1) + jnp.roll(low, -1)
    base = qsize // ATOM_Q
    extra = qsize % ATOM_Q
    place = jnp.arange(ATOM_Q, dtype=jnp.int32)
    degree = base[:, None] + (place[None, :] < extra[:, None]).astype(jnp.int32)
    signs = jax.random.randint(keys[4], (nquart, ATOM_Q // 2), 0, 2) * 2 - 1
    amount = jax.random.randint(keys[5], (nquart, ATOM_Q // 2), 0, 3)
    change = jnp.stack([signs * amount, -signs * amount], axis=-1).reshape(nquart, ATOM_Q)
    degree = (degree + change).reshape(NATOM)
    scores = jax.random.randint(keys[6], (NATOM, ncand), 0, 1048576) * ncand + jnp.arange(ncand, dtype=jnp.int32)[None, :]
    order = jnp.argsort(scores, axis=1).astype(jnp.int32)
    qstart = jnp.cumsum(qsize) - qsize
    atom_start = jnp.cumsum(degree) - degree
    slot = jnp.arange(E_DEV, dtype=jnp.int32)[None, :]
    device = jnp.arange(nquart, dtype=jnp.int32)[:, None]
    before = (device - 1) % nquart
    after = (device + 1) % nquart
    low_d = low[:, None]
    own_d = own[:, None]
    from_before = qstart[before] + qsize[before] - low_d + slot
    from_mine = qstart[device] + high[before] + (slot - low_d)
    from_after = qstart[after] + (slot - low_d - own_d)
    position = jnp.where(slot < low_d, from_before, jnp.where(slot < low_d + own_d, from_mine, from_after)).reshape(-1)
    atom = (jnp.searchsorted(atom_start, position, side='right') - 1).astype(jnp.int32)
    rank = position - atom_start[atom]
    cand = order[atom, rank]
    tile = atom // TILE_ATOMS
    target = (tile - BAND + cand // TILE_ATOMS) % ntiles * TILE_ATOMS + cand % TILE_ATOMS
    return (atom.astype(jnp.int32), target.astype(jnp.int32))


def draw_edge_src(key, part):
    return edge_lists(key)[0]


def draw_edge_dst(key, part):
    return edge_lists(key)[1]


def set_ends(values, rng, low, high):
    longest = values.shape.index(max(values.shape))
    spots = []
    for shift in (0, 1):
        where = [jax.random.randint(jax.random.fold_in(rng, axis), (), 0, length) for axis, length in enumerate(values.shape)]
        where[longest] = (where[longest] + shift) % values.shape[longest]
        spots.append(tuple(where))
    return values.at[spots[0]].set(low).at[spots[1]].set(high)


def level_of(stream_key, extent, shards, smallest, high):
    gain = 1.0
    for dim, parts in shards:
        heights = jax.random.uniform(jax.random.fold_in(jax.random.fold_in(stream_key, 6), dim), (parts,), jnp.float32, smallest / len(shards), high / len(shards))
        gain = gain * jnp.repeat(jnp.exp(heights), extent[dim] // parts).reshape((-1,) + (1,) * (len(extent) - 1 - dim))
    return gain


def noise(stream_key, dims, spread, bound, cuts=(), held_as=jnp.bfloat16):
    loudness = level_of(stream_key, dims, cuts, -0.22, 0.18) if cuts else 1.0
    values = jax.random.normal(stream_key, dims, jnp.float32) * spread * loudness
    return jnp.minimum(jnp.maximum(values, -bound), bound).astype(held_as)


def setup_inputs(seed: int = 0) -> dict:
    seeds = jax.random.split(jax.random.key(seed), 10)
    return {
        "features": noise(seeds[0], (EDGES, FEAT), 1.0, 6.0, ((0, 512),)),
        "edge_src": draw_edge_src(jax.random.fold_in(seeds[9], 71), 0),
        "edge_dst": draw_edge_dst(jax.random.fold_in(seeds[9], 71), 0),
        "edge_cell": set_ends(jax.random.randint(seeds[3], (EDGES,), 0, 3), jax.random.fold_in(seeds[3], 1), 0, 2).astype(jnp.int32),
        "cell_bias": noise(seeds[4], (3, 2 * HID), 1.0, 4.0),
        "w_in": noise(seeds[5], (FEAT, 2 * HID), FEAT ** -0.5, 0.375),
        "w_out": noise(seeds[6], (HID, ORB * ORB), (HID * ORB * NEIGH * 5) ** -0.5, 0.0068359375),
        "vectors": noise(seeds[7], (VEC, NROWS), 1.0, 6.0, ((0, 4), (1, 128)), jnp.float32),
        "cheb_coef": jnp.clip(jax.random.uniform(seeds[8], (STEPS + 1,), jnp.float32, 0.5, 1.5), 0.5, 1.5),
    }


def pair_blocks(feat, cell, cell_bias, w_in, w_out):
    pre = jnp.dot(feat, w_in, preferred_element_type=jnp.float32) + cell_bias[cell].astype(jnp.float32)
    hidden = (jax.nn.silu(pre[:, :HID]) * pre[:, HID:]).astype(jnp.bfloat16)
    return jnp.dot(hidden, w_out, preferred_element_type=jnp.float32).astype(jnp.bfloat16)


def reference(features, edge_src, edge_dst, edge_cell, cell_bias, w_in, w_out, vectors, cheb_coef):
    groups = EDGES // E_DEV

    def one_group(pieces):
        return pair_blocks(pieces[0], pieces[1], cell_bias, w_in, w_out)

    blocks = lax.map(one_group, (features.reshape(groups, E_DEV, FEAT), edge_cell.reshape(groups, E_DEV)))
    blocks = blocks.reshape(EDGES, ORB, ORB)
    ntiles = NATOM // TILE_ATOMS
    nband = 2 * BAND + 1
    tile_size = TILE_ATOMS * ORB
    src_tile = edge_src // TILE_ATOMS
    shift_tile = (edge_dst // TILE_ATOMS - src_tile + BAND) % ntiles
    flat = ((src_tile * nband + shift_tile) * TILE_ATOMS + edge_src % TILE_ATOMS) * TILE_ATOMS + edge_dst % TILE_ATOMS
    band = jnp.zeros((ntiles * nband * TILE_ATOMS * TILE_ATOMS, ORB, ORB), jnp.bfloat16).at[flat.astype(jnp.int32)].add(blocks)
    band = band.reshape(ntiles, nband, TILE_ATOMS, TILE_ATOMS, ORB, ORB).transpose(0, 1, 2, 4, 3, 5)
    band = band.reshape(ntiles, nband, tile_size, tile_size)

    def apply(field):
        field3 = field.reshape(VEC, ntiles, tile_size)
        total = jnp.zeros((VEC, ntiles, tile_size), jnp.float32)
        for diag in range(nband):
            moved = jnp.roll(field3, -(diag - BAND), axis=1)
            total = total + jnp.einsum("vtc,trc->vtr", moved, band[:, diag].astype(jnp.float32), precision=lax.Precision.HIGHEST)
        return total.reshape(VEC, NROWS)

    previous = vectors
    current = apply(previous)
    result = cheb_coef[0] * previous + cheb_coef[1] * current
    for step in range(2, STEPS + 1):
        following = 2.0 * apply(current) - previous
        result = result + cheb_coef[step] * following
        previous, current = current, following
    return result
```

```python
import functools

import jax
import jax.numpy as jnp
from jax import lax
from jax.experimental import pallas as pl
from jax.experimental.pallas import tpu as pltpu
from jax.sharding import PartitionSpec as P

MESH = pl.DeviceIdType.MESH
BF16 = jnp.bfloat16
F32 = jnp.float32

ORB = 16
TILE_ATOMS = 8
BAND = 3
NBAND = 2 * BAND + 1
HID = 256
VEC = 128
STEPS = 4
ATOM_Q = 32
SPILL = 320
E_DEV = 1280
TILE = TILE_ATOMS * ORB
TROWS = ATOM_Q // TILE_ATOMS
OWN = TROWS * TILE
HALO = BAND * TILE
WIDE = OWN + 2 * HALO
LANES = 128
IDROWS = E_DEV // LANES
SLOTS_I = TROWS * NBAND * TILE_ATOMS
ENDS = 384
PAD = ENDS - SPILL
GROUPS = 2
GROWS = VEC // GROUPS


def kernel(
    nrows, nedges,
    feat, src, dst, cell, bias, w_in, w_out, vec, coef,
    out,
    fown, fends, ids_own, ids_low, ids_high, bias_v, bias8, win_v, wout_v, wperm, vec_v, vsend,
    slots, blk, cmat, ht32, ht, tw, tf, res,
    loc_sem, ids_send, ids_recv, feat_send, feat_recv, a2a_send, a2a_recv,
    halo_send, halo_recv, fin_send, fin_recv,
):
    r = lax.axis_index("rows")
    x = lax.axis_index("edges")
    quarter = r * nedges + x
    ntiles = nrows * nedges * TROWS
    own_vecs = VEC // nedges

    up_x = lax.rem(x + 1, nedges)
    up_r = lax.rem(r + (x + 1) // nedges, nrows)
    down_x = lax.rem(x + nedges - 1, nedges)
    down_r = lax.rem(r + nrows - 1 + (x + nedges - 1) // nedges, nrows)
    up = (up_r, up_x)
    down = (down_r, down_x)

    def remote(source, target, send, recv, device):
        return pltpu.make_async_remote_copy(
            src_ref=source, dst_ref=target, send_sem=send, recv_sem=recv,
            device_id=device, device_id_type=MESH,
        )

    loads = [
        pltpu.make_async_copy(vec, vec_v, loc_sem.at[0]),
        pltpu.make_async_copy(w_out, wout_v, loc_sem.at[1]),
        pltpu.make_async_copy(w_in, win_v, loc_sem.at[2]),
        pltpu.make_async_copy(bias, bias_v, loc_sem.at[3]),
        pltpu.make_async_copy(feat, fown, loc_sem.at[4]),
        pltpu.make_async_copy(src, ids_own.at[0], loc_sem.at[5]),
        pltpu.make_async_copy(dst, ids_own.at[1], loc_sem.at[6]),
        pltpu.make_async_copy(cell, ids_own.at[2], loc_sem.at[7]),
    ]
    for load in loads:
        load.start()

    barrier = pltpu.get_barrier_semaphore()
    peers = [up, down] + [(r, lax.rem(x + off, nedges)) for off in range(1, nedges)]
    for peer in peers:
        pl.semaphore_signal(barrier, inc=1, device_id=peer, device_id_type=MESH)

    loads[0].wait()
    vsend[...] = vec_v[...].astype(BF16)
    own_cols = pl.ds(pl.multiple_of(x * OWN, OWN), OWN)
    own_rows = pl.ds(pl.multiple_of(x * own_vecs, own_vecs), own_vecs)
    tw[0, own_rows, HALO : HALO + OWN] = vec_v[:, own_cols].astype(BF16)
    fends[0:PAD, :] = jnp.zeros((PAD, HID), BF16)
    fends[2 * ENDS - PAD : 2 * ENDS, :] = jnp.zeros((PAD, HID), BF16)

    pl.semaphore_wait(barrier, len(peers))

    id_copies = []
    for n, ref in enumerate((src, dst, cell)):
        id_copies.append(remote(ref, ids_low.at[n], ids_send.at[0, n], ids_recv.at[0, n], up))
        id_copies.append(remote(ref, ids_high.at[n], ids_send.at[1, n], ids_recv.at[1, n], down))
    feat_copies = [
        remote(feat.at[E_DEV - SPILL : E_DEV], fends.at[PAD:ENDS], feat_send.at[0], feat_recv.at[0], up),
        remote(feat.at[0:SPILL], fends.at[ENDS : ENDS + SPILL], feat_send.at[1], feat_recv.at[1], down),
    ]
    for copy in id_copies + feat_copies:
        copy.start()
    a2a_copies = []
    for off in range(1, nedges):
        to = lax.rem(x + off, nedges)
        cols = pl.ds(pl.multiple_of(to * OWN, OWN), OWN)
        a2a_copies.append(
            remote(
                vsend.at[:, cols], tw.at[0, own_rows, HALO : HALO + OWN],
                a2a_send.at[off], a2a_recv.at[off], (r, to),
            )
        )
    for copy in a2a_copies:
        copy.start()

    loads[1].wait()
    k_id = lax.broadcasted_iota(jnp.int32, (HID, HID), 0)
    n_id = lax.broadcasted_iota(jnp.int32, (HID, HID), 1)
    swap = jnp.logical_and(n_id // ORB == k_id % ORB, n_id % ORB == k_id // ORB)
    perm = jnp.where(swap, 1.0, 0.0).astype(BF16)
    wperm[...] = jnp.dot(wout_v[...], perm, preferred_element_type=F32).astype(BF16)
    for load in loads[2:]:
        load.wait()
    bias8[...] = jnp.zeros_like(bias8)
    bias8[0:3, :] = bias_v[...].astype(F32)

    sub8 = lax.broadcasted_iota(jnp.int32, (8, LANES), 0)

    def pair_net(features, cell_rows, target):
        onehot = jnp.concatenate(
            [jnp.where(row == sub8, 1.0, 0.0) for row in cell_rows], axis=1
        )
        pre = jnp.dot(features, win_v[...], preferred_element_type=F32)
        pre = pre + lax.dot_general(
            onehot.astype(BF16), bias8[...].astype(BF16), (((0,), (0,)), ((), ())),
            preferred_element_type=F32,
        )
        gate = pre[:, :HID]
        hidden = (0.5 * gate * (1.0 + jnp.tanh(0.5 * gate)) * pre[:, HID:]).astype(BF16)
        target[...] = jnp.dot(hidden, wperm[...], preferred_element_type=F32).astype(BF16)

    def slot_ids(ids):
        source = ids[0]
        goal = ids[1]
        local = source % ATOM_Q
        shift = goal // TILE_ATOMS - source // TILE_ATOMS + BAND
        shift = jnp.where(shift < 0, shift + ntiles, shift)
        shift = jnp.where(shift >= ntiles, shift - ntiles, shift)
        slot = (
            (local % TILE_ATOMS) * SLOTS_I
            + (local // TILE_ATOMS * NBAND + shift) * TILE_ATOMS
            + goal % TILE_ATOMS
        )
        return jnp.where(source // ATOM_Q == quarter, slot, -1)

    for c in range(IDROWS // 2):
        rows = slice(2 * c * LANES, (2 * c + 2) * LANES)
        cell_rows = [ids_own[2, n : n + 1, :] for n in (2 * c, 2 * c + 1)]
        pair_net(fown[rows, :], cell_rows, blk.at[rows])
    own_slots = slot_ids(ids_own)
    for c in range(IDROWS):
        slots[:, c * LANES : (c + 1) * LANES] = own_slots[c : c + 1, :]

    place = lax.broadcasted_iota(jnp.int32, (SLOTS_I, 1), 0)

    def choose(i, start, count):
        row = slots[:, start : start + count] - i * SLOTS_I
        onehot = jnp.where(row == place, 1.0, 0.0).astype(BF16)
        return jnp.dot(onehot, blk[start : start + count, :], preferred_element_type=F32)

    @pl.loop(0, TILE_ATOMS)
    def _(i):
        cmat[i] = choose(i, 0, E_DEV)

    for copy in a2a_copies:
        copy.wait_recv()

    def halo(step, group, rows):
        return [
            remote(
                tw.at[step, rows, HALO + OWN - HALO : HALO + OWN], tw.at[step, rows, 0:HALO],
                halo_send.at[step, 0, group], halo_recv.at[step, 0, group], up,
            ),
            remote(
                tw.at[step, rows, HALO : 2 * HALO], tw.at[step, rows, HALO + OWN : WIDE],
                halo_send.at[step, 1, group], halo_recv.at[step, 1, group], down,
            ),
        ]

    group_rows = [slice(g * GROWS, (g + 1) * GROWS) for g in range(GROUPS)]
    halos = {}
    for g in range(GROUPS):
        halos[0, g] = halo(0, g, group_rows[g])
        for copy in halos[0, g]:
            copy.start()

    for copy in id_copies + feat_copies:
        copy.wait_recv()
    low_slots = slot_ids(ids_low)
    high_slots = slot_ids(ids_high)
    nends = ENDS // LANES
    for c in range(nends):
        at = E_DEV + c * LANES
        slots[:, at : at + LANES] = low_slots[IDROWS - nends + c : IDROWS - nends + c + 1, :]
        at = at + ENDS
        slots[:, at : at + LANES] = high_slots[c : c + 1, :]
    end_cells = [ids_low[2, n : n + 1, :] for n in range(IDROWS - nends, IDROWS)]
    end_cells += [ids_high[2, n : n + 1, :] for n in range(nends)]
    for c in range(nends):
        rows = slice(2 * c * LANES, (2 * c + 2) * LANES)
        target = blk.at[E_DEV + 2 * c * LANES : E_DEV + (2 * c + 2) * LANES]
        pair_net(fends[rows, :], end_cells[2 * c : 2 * c + 2], target)

    @pl.loop(0, TILE_ATOMS)
    def _(i):
        cmat[i] = cmat[i] + choose(i, E_DEV, 2 * ENDS)

    lane = lax.broadcasted_iota(jnp.int32, (8, LANES), 1)

    @pl.loop(0, TROWS * NBAND)
    def _(td):
        start = td * TILE
        rows = pl.ds(pl.multiple_of(td * 8, 8), 8)
        for half in range(2):
            parts = [cmat[i, rows, half * LANES : (half + 1) * LANES] for i in range(8)]
            for bit in range(3):
                width = ORB << bit
                high_lane = (lane // width) % 2 == 1
                for n in range(8):
                    if n & (1 << bit):
                        continue
                    m = n | (1 << bit)
                    first = jnp.where(high_lane, pltpu.roll(parts[m], width, 1), parts[n])
                    second = jnp.where(high_lane, parts[m], pltpu.roll(parts[n], LANES - width, 1))
                    parts[n], parts[m] = first, second
            for n in range(8):
                ht32[pl.ds(start + half * 8 + n, 8, stride=ORB), :] = parts[n]

    for pair in range(TROWS // 2):
        ht[pair, NBAND * TILE : (NBAND + 1) * TILE, 0:TILE] = jnp.zeros((TILE, TILE), BF16)
        ht[pair, 0:TILE, TILE : 2 * TILE] = jnp.zeros((TILE, TILE), BF16)
        for a in range(2):
            t = 2 * pair + a
            piece = ht32[t * NBAND * TILE : (t + 1) * NBAND * TILE, :].astype(BF16)
            ht[pair, a * TILE : (a + NBAND) * TILE, a * TILE : (a + 1) * TILE] = piece

    finals = []
    for step in range(1, STEPS + 1):
        for g in range(GROUPS):
            rows = group_rows[g]
            for copy in halos[step - 1, g]:
                copy.wait_recv()
            for pair in range(TROWS // 2):
                cols = slice(pair * 2 * TILE, (pair + 1) * 2 * TILE)
                wide = slice(pair * 2 * TILE, pair * 2 * TILE + (NBAND + 1) * TILE)
                product = jnp.dot(tw[step - 1, rows, wide], ht[pair], preferred_element_type=F32)
                mid = slice(HALO + pair * 2 * TILE, HALO + (pair + 1) * 2 * TILE)
                if step == 1:
                    new = product
                    total = coef[0] * tw[0, rows, mid].astype(F32) + coef[1] * new
                else:
                    if step == 2:
                        older = tw[0, rows, mid].astype(F32)
                    else:
                        older = tf[step - 3, rows, cols]
                    new = 2.0 * product - older
                    total = res[rows, cols] + coef[step] * new
                if step < STEPS:
                    tw[step, rows, mid] = new.astype(BF16)
                if step < STEPS - 1:
                    tf[step - 1, rows, cols] = new
                if step < STEPS:
                    res[rows, cols] = total
                else:
                    fsend = tw.at[STEPS]
                    fsend[rows, cols] = total.astype(BF16)
            if step < STEPS:
                halos[step, g] = halo(step, g, rows)
                for copy in halos[step, g]:
                    copy.start()
            else:
                for owner in range(g * GROWS // own_vecs, (g + 1) * GROWS // own_vecs):
                    vecs = slice(owner * own_vecs, (owner + 1) * own_vecs)
                    copy = remote(
                        tw.at[STEPS, vecs, 0:OWN], out.at[:, own_cols],
                        fin_send.at[owner], fin_recv.at[x], (r, owner),
                    )
                    finals.append(copy)

                    @pl.when(x != owner)
                    def _(copy=copy):
                        copy.start()

                    @pl.when(x == owner)
                    def _(vecs=vecs):
                        out[:, own_cols] = tw[STEPS, vecs, 0:OWN]

    for copy in id_copies + feat_copies + a2a_copies:
        copy.wait_send()
    for pair in halos.values():
        for copy in pair:
            copy.wait_send()
    for owner in range(nedges):

        @pl.when(x != owner)
        def _(owner=owner):
            finals[owner].wait_send()
            remote(
                tw.at[STEPS, 0:own_vecs, 0:OWN], out.at[:, owner * OWN : (owner + 1) * OWN],
                fin_send.at[owner], fin_recv.at[owner], (r, owner),
            ).wait_recv()


def per_device(nrows, nedges, features, edge_src, edge_dst, edge_cell, cell_bias, w_in, w_out, vectors, cheb_coef):
    ids = [a.reshape(IDROWS, LANES) for a in (edge_src, edge_dst, edge_cell)]
    own_vecs = VEC // nedges
    dma = pltpu.SemaphoreType.DMA
    anywhere = pl.BlockSpec(memory_space=pl.ANY)
    result = pl.pallas_call(
        functools.partial(kernel, nrows, nedges),
        out_shape=jax.ShapeDtypeStruct(vectors.shape, BF16),
        in_specs=[anywhere] * 8 + [pl.BlockSpec(memory_space=pltpu.SMEM)],
        out_specs=pl.BlockSpec(memory_space=pltpu.VMEM),
        scratch_shapes=[
            pltpu.VMEM((E_DEV, HID), BF16),
            pltpu.VMEM((2 * ENDS, HID), BF16),
            pltpu.VMEM((3, IDROWS, LANES), jnp.int32),
            pltpu.VMEM((3, IDROWS, LANES), jnp.int32),
            pltpu.VMEM((3, IDROWS, LANES), jnp.int32),
            pltpu.VMEM((3, 2 * HID), BF16),
            pltpu.VMEM((8, 2 * HID), F32),
            pltpu.VMEM((HID, 2 * HID), BF16),
            pltpu.VMEM((HID, HID), BF16),
            pltpu.VMEM((HID, HID), BF16),
            pltpu.VMEM(vectors.shape, F32),
            pltpu.VMEM(vectors.shape, BF16),
            pltpu.VMEM((1, E_DEV + 2 * ENDS), jnp.int32),
            pltpu.VMEM((E_DEV + 2 * ENDS, HID), BF16),
            pltpu.VMEM((TILE_ATOMS, SLOTS_I, HID), F32),
            pltpu.VMEM((TROWS * NBAND * TILE, TILE), F32),
            pltpu.VMEM((TROWS // 2, (NBAND + 1) * TILE, 2 * TILE), BF16),
            pltpu.VMEM((STEPS + 1, VEC, WIDE), BF16),
            pltpu.VMEM((STEPS - 2, VEC, OWN), F32),
            pltpu.VMEM((VEC, OWN), F32),
            dma((8,)),
            dma((2, 3)),
            dma((2, 3)),
            dma((2,)),
            dma((2,)),
            dma((nedges,)),
            dma((nedges,)),
            dma((STEPS, 2, GROUPS)),
            dma((STEPS, 2, GROUPS)),
            dma((nedges,)),
            dma((nedges,)),
        ],
        compiler_params=pltpu.CompilerParams(
            collective_id=0, has_side_effects=True
        ),
        name="filter",
    )(features, *ids, cell_bias, w_in, w_out, vectors, cheb_coef)
    return result.astype(F32)


def solution(mesh):
    nrows, nedges = mesh.shape["rows"], mesh.shape["edges"]
    placed = (
        P(("rows", "edges"), None),
        P(("rows", "edges")),
        P(("rows", "edges")),
        P(("rows", "edges")),
        P(),
        P(),
        P(),
        P("edges", "rows"),
        P(),
    )
    return jax.shard_map(
        functools.partial(per_device, nrows, nedges),
        mesh=mesh,
        in_specs=placed,
        out_specs=P("edges", "rows"),
        check_vma=False,
    )
```

```python
import functools

import jax
import jax.numpy as jnp
from jax import lax
from jax.experimental import pallas as pl
from jax.experimental.pallas import tpu as pltpu
from jax.sharding import PartitionSpec as P

MESH = pl.DeviceIdType.MESH
BF16 = jnp.bfloat16
F32 = jnp.float32

ORB = 16
TILE_ATOMS = 8
BAND = 3
NBAND = 2 * BAND + 1
HID = 256
VEC = 128
STEPS = 4
ATOM_Q = 32
SPILL = 320
E_DEV = 1280
TILE = TILE_ATOMS * ORB
TROWS = ATOM_Q // TILE_ATOMS
OWN = TROWS * TILE
HALO = BAND * TILE
WIDE = OWN + 2 * HALO
LANES = 128
IDROWS = E_DEV // LANES
PAIRS = TROWS // 2
SLOTS_I = 2 * NBAND * TILE_ATOMS
SLOTS = TILE_ATOMS * SLOTS_I
ENDS = 384
PAD = ENDS - SPILL
GROUPS = 2
GROWS = VEC // GROUPS


def kernel(
    nrows, nedges,
    feat, src, dst, cell, bias, w_in, w_out, vec, coef,
    out,
    fown, fends, ids_own, ids_low, ids_high, bias_v, coef_s, win_v, wout_v, wperm, vec_v, vsend,
    slots, cells, onehot_ends, blk, cmat, ht32, ht, tw, tf, res,
    loc_sem, ids_send, ids_recv, feat_send, feat_recv, win_send, win_recv, rim_send, rim_recv,
    halo_send, halo_recv, fin_send, fin_recv,
):
    r = lax.axis_index("rows")
    x = lax.axis_index("edges")
    quarter = r * nedges + x
    ntiles = nrows * nedges * TROWS
    own_vecs = VEC // nedges

    up_x = lax.rem(x + 1, nedges)
    up_r = lax.rem(r + (x + 1) // nedges, nrows)
    down_x = lax.rem(x + nedges - 1, nedges)
    down_r = lax.rem(r + nrows - 1 + (x + nedges - 1) // nedges, nrows)
    up = (up_r, up_x)
    down = (down_r, down_x)

    def remote(source, target, send, recv, device):
        return pltpu.make_async_remote_copy(
            src_ref=source, dst_ref=target, send_sem=send, recv_sem=recv,
            device_id=device, device_id_type=MESH,
        )

    loads = [
        pltpu.make_async_copy(vec, vec_v, loc_sem.at[0]),
        pltpu.make_async_copy(w_out, wout_v, loc_sem.at[1]),
        pltpu.make_async_copy(w_in, win_v, loc_sem.at[2]),
        pltpu.make_async_copy(bias, bias_v, loc_sem.at[3]),
        pltpu.make_async_copy(feat, fown, loc_sem.at[4]),
        pltpu.make_async_copy(src, ids_own.at[0], loc_sem.at[5]),
        pltpu.make_async_copy(dst, ids_own.at[1], loc_sem.at[6]),
        pltpu.make_async_copy(cell, ids_own.at[2], loc_sem.at[7]),
        pltpu.make_async_copy(coef, coef_s, loc_sem.at[8]),
    ]
    for load in loads:
        load.start()

    barrier = pltpu.get_barrier_semaphore()
    after_r = lax.rem(r + 1, nrows)
    before_r = lax.rem(r + nrows - 1, nrows)

    def greet(device):
        pl.semaphore_signal(barrier, inc=1, device_id=device, device_id_type=MESH)

    for device in [up, down] + [(r, lax.rem(x + off, nedges)) for off in range(1, nedges)]:
        greet(device)

    @pl.when(x == 0)
    def _():
        for n in range(nedges):
            greet((before_r, n))

    @pl.when(x == nedges - 1)
    def _():
        for n in range(nedges):
            greet((after_r, n))

    loads[0].wait()
    vsend[...] = vec_v[...].astype(BF16)
    own_cols = pl.ds(pl.multiple_of(x * OWN, OWN), OWN)
    own_rows = pl.ds(pl.multiple_of(x * own_vecs, own_vecs), own_vecs)
    fends[0:PAD, :] = jnp.zeros((PAD, HID), BF16)
    fends[2 * ENDS - PAD : 2 * ENDS, :] = jnp.zeros((PAD, HID), BF16)

    pl.semaphore_wait(barrier, nedges + 3)

    id_copies = []
    for n, ref in enumerate((src, dst, cell)):
        id_copies.append(remote(ref, ids_low.at[n], ids_send.at[0, n], ids_recv.at[0, n], up))
        id_copies.append(remote(ref, ids_high.at[n], ids_send.at[1, n], ids_recv.at[1, n], down))
    feat_copies = [
        remote(feat.at[E_DEV - SPILL : E_DEV], fends.at[PAD:ENDS], feat_send.at[0], feat_recv.at[0], up),
        remote(feat.at[0:SPILL], fends.at[ENDS : ENDS + SPILL], feat_send.at[1], feat_recv.at[1], down),
    ]
    for copy in id_copies + feat_copies:
        copy.start()
    loads[1].wait()
    k_id = lax.broadcasted_iota(jnp.int32, (HID, HID), 0)
    n_id = lax.broadcasted_iota(jnp.int32, (HID, HID), 1)
    swap = jnp.logical_and(n_id // ORB == k_id % ORB, n_id % ORB == k_id // ORB)
    perm = jnp.where(swap, 1.0, 0.0).astype(BF16)
    wperm[...] = jnp.dot(wout_v[...], perm, preferred_element_type=F32).astype(BF16)
    for load in loads[2:]:
        load.wait()
    half = jnp.where(lax.broadcasted_iota(jnp.int32, (1, 2 * HID), 1) < HID, 0.5, 1.0)
    win_v[...] = (win_v[...].astype(F32) * half).astype(BF16)
    bias_of = [bias_v[n : n + 1, :].astype(F32) * half for n in range(3)]

    def spread_cells(row, at):
        cells[at : at + LANES, :] = jnp.broadcast_to(row.astype(F32), (LANES, LANES)).T

    def pair_net(features, at):
        rows = slice(at, at + 2 * LANES)
        kind = cells[rows, :]
        second, third = kind > 0.5, kind > 1.5
        pre = jnp.dot(features, win_v[...], preferred_element_type=F32)
        parts = []
        for c in range(0, 2 * HID, LANES):
            b0, b1, b2 = [b[:, c : c + LANES] for b in bias_of]
            parts.append(pre[:, c : c + LANES] + jnp.where(third, b2, jnp.where(second, b1, b0)))
        hidden = []
        for n in range(HID // LANES):
            gate = parts[n]
            hidden.append(((gate + gate * jnp.tanh(gate)) * parts[n + HID // LANES]).astype(BF16))
        hidden = jnp.concatenate(hidden, axis=1)
        blk[rows, :] = jnp.dot(hidden, wperm[...], preferred_element_type=F32).astype(BF16)

    def slot_ids(ids):
        source = ids[0]
        goal = ids[1]
        local = source % ATOM_Q
        shift = goal // TILE_ATOMS - source // TILE_ATOMS + BAND
        shift = jnp.where(shift < 0, shift + ntiles, shift)
        shift = jnp.where(shift >= ntiles, shift - ntiles, shift)
        tile = local // TILE_ATOMS
        slot = (
            tile // 2 * SLOTS
            + (local % TILE_ATOMS) * SLOTS_I
            + (tile % 2 * NBAND + shift) * TILE_ATOMS
            + goal % TILE_ATOMS
        )
        return jnp.where(source // ATOM_Q == quarter, slot, -1)

    for c in range(IDROWS // 2):
        at = 2 * c * LANES
        for n in range(2):
            spread_cells(ids_own[2, 2 * c + n : 2 * c + n + 1, :], at + n * LANES)
        pair_net(fown[at : at + 2 * LANES, :], at)

    windows = []
    for n in range(nedges):
        first = max(n * OWN - HALO, 0)
        last = min((n + 1) * OWN + HALO, nedges * OWN)
        at = first - (n * OWN - HALO)
        windows.append((first, last, at))

    def window(n, source):
        first, last, at = windows[n]
        rows = pl.ds(pl.multiple_of(source * own_vecs, own_vecs), own_vecs)
        return remote(
            vsend.at[:, first:last], tw.at[0, rows, at : at + last - first],
            win_send.at[n], win_recv.at[source], (r, n),
        )

    for n in range(nedges):

        @pl.when(x != n)
        def _(n=n):
            window(n, x).start()

        @pl.when(x == n)
        def _(n=n):
            first, last, at = windows[n]
            tw[0, own_rows, at : at + last - first] = vsend[:, first:last]

    def rim(side, source):
        rows = pl.ds(pl.multiple_of(source * own_vecs, own_vecs), own_vecs)
        if side == 0:
            source_cols, cols, device = slice(nedges * OWN - HALO, nedges * OWN), slice(0, HALO), (after_r, 0)
        else:
            source_cols, cols, device = slice(0, HALO), slice(HALO + OWN, WIDE), (before_r, nedges - 1)
        return remote(
            vsend.at[:, source_cols], tw.at[0, rows, cols],
            rim_send.at[side], rim_recv.at[side, source], device,
        )

    own_rims = [rim(side, x) for side in range(2)]
    for copy in own_rims:
        copy.start()

    own_slots = slot_ids(ids_own)
    for c in range(IDROWS):
        slots[:, c * LANES : (c + 1) * LANES] = own_slots[c : c + 1, :]

    place = lax.broadcasted_iota(jnp.int32, (SLOTS, 1), 0)

    @pl.loop(0, PAIRS)
    def _(pair):
        row = slots[:, 0:E_DEV] - pair * SLOTS
        onehot = jnp.where(row == place, 1.0, 0.0).astype(BF16)
        own = jnp.dot(onehot, blk[0:E_DEV, :], preferred_element_type=F32)
        cmat[pair] = own.astype(BF16)

    def halo(step, group, rows):
        return [
            remote(
                tw.at[step, rows, HALO + OWN - HALO : HALO + OWN], tw.at[step, rows, 0:HALO],
                halo_send.at[step, 0, group], halo_recv.at[step, 0, group], up,
            ),
            remote(
                tw.at[step, rows, HALO : 2 * HALO], tw.at[step, rows, HALO + OWN : WIDE],
                halo_send.at[step, 1, group], halo_recv.at[step, 1, group], down,
            ),
        ]

    group_rows = [slice(g * GROWS, (g + 1) * GROWS) for g in range(GROUPS)]
    halos = {}

    for copy in id_copies:
        copy.wait_recv()
    low_slots = slot_ids(ids_low)
    high_slots = slot_ids(ids_high)
    nends = ENDS // LANES
    for c in range(nends):
        low_row = slice(IDROWS - nends + c, IDROWS - nends + c + 1)
        high_row = slice(c, c + 1)
        at = E_DEV + c * LANES
        slots[:, at : at + LANES] = low_slots[low_row, :]
        spread_cells(ids_low[2, low_row, :], at)
        at = at + ENDS
        slots[:, at : at + LANES] = high_slots[high_row, :]
        spread_cells(ids_high[2, high_row, :], at)

    @pl.loop(0, PAIRS)
    def _(pair):
        row = slots[:, E_DEV : E_DEV + 2 * ENDS] - pair * SLOTS
        onehot_ends[pair] = jnp.where(row == place, 1.0, 0.0).astype(BF16)

    for copy in feat_copies:
        copy.wait_recv()
    for c in range(nends):
        at = 2 * c * LANES
        pair_net(fends[at : at + 2 * LANES, :], E_DEV + at)

    lane = lax.broadcasted_iota(jnp.int32, (16, LANES), 1)
    upper = [(lane & (ORB << bit)) != 0 for bit in range(3)]
    for pair in range(PAIRS):
        ends = jnp.dot(
            onehot_ends[pair], blk[E_DEV : E_DEV + 2 * ENDS, :], preferred_element_type=F32
        )
        placed = cmat[pair] + ends.astype(BF16)
        for k in range(NBAND):
            for side in range(2):
                cols = slice(side * LANES, (side + 1) * LANES)
                parts = []
                for i in range(TILE_ATOMS):
                    at = i * SLOTS_I + 16 * k
                    parts.append(placed[at : at + 16, cols])
                for bit in range(3):
                    width = ORB << bit
                    for n in range(8):
                        if n & (1 << bit):
                            continue
                        m = n | (1 << bit)
                        first = jnp.where(upper[bit], pltpu.roll(parts[m], width, 1), parts[n])
                        second = jnp.where(upper[bit], parts[m], pltpu.roll(parts[n], LANES - width, 1))
                        parts[n], parts[m] = first, second
                for n in range(8):
                    both = parts[n].astype(F32)
                    for s in range(2):
                        start = (pair * 2 * NBAND + 2 * k + s) * TILE + side * 8 + n
                        ht32[pl.ds(start, 8, stride=ORB), :] = both[8 * s : 8 * s + 8, :]
        ht[pair, NBAND * TILE : (NBAND + 1) * TILE, 0:TILE] = jnp.zeros((TILE, TILE), BF16)
        ht[pair, 0:TILE, TILE : 2 * TILE] = jnp.zeros((TILE, TILE), BF16)
        for a in range(2):
            t = 2 * pair + a
            piece = ht32[t * NBAND * TILE : (t + 1) * NBAND * TILE, :].astype(BF16)
            ht[pair, a * TILE : (a + NBAND) * TILE, a * TILE : (a + 1) * TILE] = piece

    for n in range(nedges):

        @pl.when(x == n)
        def _(n=n):
            for source in range(nedges):
                if source != n:
                    window(n, source).wait_recv()
                if n == 0:
                    rim(0, source).wait_recv()
                if n == nedges - 1:
                    rim(1, source).wait_recv()

    finals = []
    for step in range(1, STEPS + 1):
        for g in range(GROUPS):
            rows = group_rows[g]
            if step > 1:
                for copy in halos[step - 1, g]:
                    copy.wait_recv()
            for pair in range(PAIRS):
                cols = slice(pair * 2 * TILE, (pair + 1) * 2 * TILE)
                wide = slice(pair * 2 * TILE, pair * 2 * TILE + (NBAND + 1) * TILE)
                product = jnp.dot(tw[step - 1, rows, wide], ht[pair], preferred_element_type=F32)
                mid = slice(HALO + pair * 2 * TILE, HALO + (pair + 1) * 2 * TILE)
                if step == 1:
                    new = product
                    total = coef_s[0] * tw[0, rows, mid].astype(F32) + coef_s[1] * new
                else:
                    if step == 2:
                        older = tw[0, rows, mid].astype(F32)
                    else:
                        older = tf[step - 3, rows, cols]
                    new = 2.0 * product - older
                    total = res[rows, cols] + coef_s[step] * new
                if step < STEPS:
                    tw[step, rows, mid] = new.astype(BF16)
                if step < STEPS - 1:
                    tf[step - 1, rows, cols] = new
                if step < STEPS:
                    res[rows, cols] = total
                else:
                    fsend = tw.at[STEPS]
                    fsend[rows, cols] = total.astype(BF16)
            if step < STEPS:
                halos[step, g] = halo(step, g, rows)
                for copy in halos[step, g]:
                    copy.start()
            else:
                for owner in range(g * GROWS // own_vecs, (g + 1) * GROWS // own_vecs):
                    vecs = slice(owner * own_vecs, (owner + 1) * own_vecs)
                    copy = remote(
                        tw.at[STEPS, vecs, 0:OWN], out.at[:, own_cols],
                        fin_send.at[owner], fin_recv.at[x], (r, owner),
                    )
                    finals.append(copy)

                    @pl.when(x != owner)
                    def _(copy=copy):
                        copy.start()

                    @pl.when(x == owner)
                    def _(vecs=vecs):
                        out[:, own_cols] = tw[STEPS, vecs, 0:OWN]

    for copy in id_copies + feat_copies + own_rims:
        copy.wait_send()
    for n in range(nedges):

        @pl.when(x != n)
        def _(n=n):
            window(n, x).wait_send()
    for pair in halos.values():
        for copy in pair:
            copy.wait_send()
    for owner in range(nedges):

        @pl.when(x != owner)
        def _(owner=owner):
            finals[owner].wait_send()
            remote(
                tw.at[STEPS, 0:own_vecs, 0:OWN], out.at[:, owner * OWN : (owner + 1) * OWN],
                fin_send.at[owner], fin_recv.at[owner], (r, owner),
            ).wait_recv()


def per_device(nrows, nedges, features, edge_src, edge_dst, edge_cell, cell_bias, w_in, w_out, vectors, cheb_coef):
    ids = [a.reshape(IDROWS, LANES) for a in (edge_src, edge_dst, edge_cell)]
    own_vecs = VEC // nedges
    dma = pltpu.SemaphoreType.DMA
    anywhere = pl.BlockSpec(memory_space=pl.ANY)
    result = pl.pallas_call(
        functools.partial(kernel, nrows, nedges),
        out_shape=jax.ShapeDtypeStruct(vectors.shape, BF16),
        in_specs=[anywhere] * 9,
        out_specs=pl.BlockSpec(memory_space=pltpu.VMEM),
        scratch_shapes=[
            pltpu.VMEM((E_DEV, HID), BF16),
            pltpu.VMEM((2 * ENDS, HID), BF16),
            pltpu.VMEM((3, IDROWS, LANES), jnp.int32),
            pltpu.VMEM((3, IDROWS, LANES), jnp.int32),
            pltpu.VMEM((3, IDROWS, LANES), jnp.int32),
            pltpu.VMEM((3, 2 * HID), BF16),
            pltpu.SMEM((STEPS + 1,), F32),
            pltpu.VMEM((HID, 2 * HID), BF16),
            pltpu.VMEM((HID, HID), BF16),
            pltpu.VMEM((HID, HID), BF16),
            pltpu.VMEM(vectors.shape, F32),
            pltpu.VMEM(vectors.shape, BF16),
            pltpu.VMEM((1, E_DEV + 2 * ENDS), jnp.int32),
            pltpu.VMEM((E_DEV + 2 * ENDS, LANES), F32),
            pltpu.VMEM((PAIRS, SLOTS, 2 * ENDS), BF16),
            pltpu.VMEM((E_DEV + 2 * ENDS, HID), BF16),
            pltpu.VMEM((PAIRS, SLOTS, HID), BF16),
            pltpu.VMEM((TROWS * NBAND * TILE, TILE), F32),
            pltpu.VMEM((PAIRS, (NBAND + 1) * TILE, 2 * TILE), BF16),
            pltpu.VMEM((STEPS + 1, VEC, WIDE), BF16),
            pltpu.VMEM((STEPS - 2, VEC, OWN), F32),
            pltpu.VMEM((VEC, OWN), F32),
            dma((9,)),
            dma((2, 3)),
            dma((2, 3)),
            dma((2,)),
            dma((2,)),
            dma((nedges,)),
            dma((nedges,)),
            dma((2,)),
            dma((2, nedges)),
            dma((STEPS, 2, GROUPS)),
            dma((STEPS, 2, GROUPS)),
            dma((nedges,)),
            dma((nedges,)),
        ],
        compiler_params=pltpu.CompilerParams(
            collective_id=0, has_side_effects=True
        ),
        name="filter",
    )(features, *ids, cell_bias, w_in, w_out, vectors, cheb_coef)
    return result.astype(F32)


def solution(mesh):
    nrows, nedges = mesh.shape["rows"], mesh.shape["edges"]
    placed = (
        P(("rows", "edges"), None),
        P(("rows", "edges")),
        P(("rows", "edges")),
        P(("rows", "edges")),
        P(),
        P(),
        P(),
        P("edges", "rows"),
        P(),
    )
    return jax.shard_map(
        functools.partial(per_device, nrows, nedges),
        mesh=mesh,
        in_specs=placed,
        out_specs=P("edges", "rows"),
        check_vma=False,
    )
```

```python
import functools

import jax
import jax.numpy as jnp
from jax import lax
from jax.experimental import pallas as pl
from jax.experimental.pallas import tpu as pltpu
from jax.sharding import PartitionSpec as P

MESH = pl.DeviceIdType.MESH
BF16 = jnp.bfloat16
F32 = jnp.float32

ORB = 16
TILE_ATOMS = 8
BAND = 3
NBAND = 2 * BAND + 1
HID = 256
VEC = 128
STEPS = 4
ATOM_Q = 32
SPILL = 320
E_DEV = 1280
TILE = TILE_ATOMS * ORB
TROWS = ATOM_Q // TILE_ATOMS
OWN = TROWS * TILE
HALO = BAND * TILE
WIDE = OWN + 2 * HALO
LANES = 128
IDROWS = E_DEV // LANES
PAIRS = TROWS // 2
SLOTS_I = 2 * NBAND * TILE_ATOMS
SLOTS = TILE_ATOMS * SLOTS_I
ENDS = 384
PAD = ENDS - SPILL
GROUPS = 2
GROWS = VEC // GROUPS


def kernel(
    nrows, nedges,
    feat, src, dst, cell, bias, w_in, w_out, vec, coef,
    out,
    fown, fends, ids_own, ids_low, ids_high, bias_v, coef_s, win_v, wout_v, wperm, vec_v, vsend,
    slots, cells, onehot_ends, hid, blk, cmat, ht32, ht, tw, tf, res,
    loc_sem, ids_send, ids_recv, feat_send, feat_recv, win_send, win_recv, rim_send, rim_recv,
    halo_send, halo_recv, fin_send, fin_recv,
):
    r = lax.axis_index("rows")
    x = lax.axis_index("edges")
    quarter = r * nedges + x
    ntiles = nrows * nedges * TROWS
    own_vecs = VEC // nedges

    up_x = lax.rem(x + 1, nedges)
    up_r = lax.rem(r + (x + 1) // nedges, nrows)
    down_x = lax.rem(x + nedges - 1, nedges)
    down_r = lax.rem(r + nrows - 1 + (x + nedges - 1) // nedges, nrows)
    up = (up_r, up_x)
    down = (down_r, down_x)

    def remote(source, target, send, recv, device):
        return pltpu.make_async_remote_copy(
            src_ref=source, dst_ref=target, send_sem=send, recv_sem=recv,
            device_id=device, device_id_type=MESH,
        )

    loads = [
        pltpu.make_async_copy(vec, vec_v, loc_sem.at[0]),
        pltpu.make_async_copy(w_out, wout_v, loc_sem.at[1]),
        pltpu.make_async_copy(w_in, win_v, loc_sem.at[2]),
        pltpu.make_async_copy(bias, bias_v, loc_sem.at[3]),
        pltpu.make_async_copy(feat, fown, loc_sem.at[4]),
        pltpu.make_async_copy(src, ids_own.at[0], loc_sem.at[5]),
        pltpu.make_async_copy(dst, ids_own.at[1], loc_sem.at[6]),
        pltpu.make_async_copy(cell, ids_own.at[2], loc_sem.at[7]),
        pltpu.make_async_copy(coef, coef_s, loc_sem.at[8]),
    ]
    for load in loads:
        load.start()

    barrier = pltpu.get_barrier_semaphore()
    after_r = lax.rem(r + 1, nrows)
    before_r = lax.rem(r + nrows - 1, nrows)

    def greet(device):
        pl.semaphore_signal(barrier, inc=1, device_id=device, device_id_type=MESH)

    for device in [up, down] + [(r, lax.rem(x + off, nedges)) for off in range(1, nedges)]:
        greet(device)

    @pl.when(x == 0)
    def _():
        for n in range(nedges):
            greet((before_r, n))

    @pl.when(x == nedges - 1)
    def _():
        for n in range(nedges):
            greet((after_r, n))

    loads[1].wait()
    k_id = lax.broadcasted_iota(jnp.int32, (HID, HID), 0)
    n_id = lax.broadcasted_iota(jnp.int32, (HID, HID), 1)
    swap = jnp.logical_and(n_id // ORB == k_id % ORB, n_id % ORB == k_id // ORB)
    perm = jnp.where(swap, 1.0, 0.0).astype(BF16)
    wperm[...] = jnp.dot(wout_v[...], perm, preferred_element_type=F32).astype(BF16)
    for load in loads[2:]:
        load.wait()
    half = jnp.where(lax.broadcasted_iota(jnp.int32, (1, 2 * HID), 1) < HID, 0.5, 1.0)
    win_v[...] = (win_v[...].astype(F32) * half).astype(BF16)
    bias_of = [bias_v[n : n + 1, :].astype(F32) * half for n in range(3)]

    def pair_net(at, count):
        for n in range(at, at + count, LANES):
            row = ids_own[2, n // LANES : n // LANES + 1, :]
            cells[n : n + LANES, :] = jnp.broadcast_to(row.astype(F32), (LANES, LANES)).T
        for first in range(at, at + count, 128):
            rows = slice(first, first + 128)
            kind = cells[rows, :]
            second, third = kind > 0.5, kind > 1.5
            pre = jnp.dot(fown[rows, :], win_v[...], preferred_element_type=F32)
            parts = []
            for c in range(0, 2 * HID, LANES):
                b0, b1, b2 = [b[:, c : c + LANES] for b in bias_of]
                parts.append(pre[:, c : c + LANES] + jnp.where(third, b2, jnp.where(second, b1, b0)))
            for n in range(HID // LANES):
                gate = parts[n]
                value = (gate + gate * jnp.tanh(gate)) * parts[n + HID // LANES]
                hid[rows, n * LANES : (n + 1) * LANES] = value.astype(BF16)
        rows = slice(at, at + count)
        blk[rows, :] = jnp.dot(hid[rows, :], wperm[...], preferred_element_type=F32).astype(BF16)

    def slot_ids(ids):
        source = ids[0]
        goal = ids[1]
        local = source % ATOM_Q
        shift = goal // TILE_ATOMS - source // TILE_ATOMS + BAND
        shift = jnp.where(shift < 0, shift + ntiles, shift)
        shift = jnp.where(shift >= ntiles, shift - ntiles, shift)
        tile = local // TILE_ATOMS
        slot = (
            tile // 2 * SLOTS
            + (local % TILE_ATOMS) * SLOTS_I
            + (tile % 2 * NBAND + shift) * TILE_ATOMS
            + goal % TILE_ATOMS
        )
        return jnp.where(source // ATOM_Q == quarter, slot, -1)

    ends_rows = (slice(0, ENDS), slice(E_DEV - ENDS, E_DEV))
    for rows in ends_rows:
        pair_net(rows.start, ENDS)

    loads[0].wait()
    vsend[...] = vec_v[...].astype(BF16)
    own_cols = pl.ds(pl.multiple_of(x * OWN, OWN), OWN)
    own_rows = pl.ds(pl.multiple_of(x * own_vecs, own_vecs), own_vecs)
    fends[0:PAD, :] = jnp.zeros((PAD, HID), BF16)
    fends[2 * ENDS - PAD : 2 * ENDS, :] = jnp.zeros((PAD, HID), BF16)

    pl.semaphore_wait(barrier, nedges + 3)

    id_copies = []
    for n, ref in enumerate((src, dst)):
        id_copies.append(remote(ref, ids_low.at[n], ids_send.at[0, n], ids_recv.at[0, n], up))
        id_copies.append(remote(ref, ids_high.at[n], ids_send.at[1, n], ids_recv.at[1, n], down))
    blk_copies = [
        remote(blk.at[E_DEV - SPILL : E_DEV], fends.at[PAD:ENDS], feat_send.at[0], feat_recv.at[0], up),
        remote(blk.at[0:SPILL], fends.at[ENDS : ENDS + SPILL], feat_send.at[1], feat_recv.at[1], down),
    ]
    for copy in id_copies + blk_copies:
        copy.start()
    pair_net(ENDS, E_DEV - 2 * ENDS)

    windows = []
    for n in range(nedges):
        first = max(n * OWN - HALO, 0)
        last = min((n + 1) * OWN + HALO, nedges * OWN)
        at = first - (n * OWN - HALO)
        windows.append((first, last, at))

    def window(n, source):
        first, last, at = windows[n]
        rows = pl.ds(pl.multiple_of(source * own_vecs, own_vecs), own_vecs)
        return remote(
            vsend.at[:, first:last], tw.at[0, rows, at : at + last - first],
            win_send.at[n], win_recv.at[source], (r, n),
        )

    def rim(side, source):
        rows = pl.ds(pl.multiple_of(source * own_vecs, own_vecs), own_vecs)
        if side == 0:
            source_cols, cols, device = slice(nedges * OWN - HALO, nedges * OWN), slice(0, HALO), (after_r, 0)
        else:
            source_cols, cols, device = slice(0, HALO), slice(HALO + OWN, WIDE), (before_r, nedges - 1)
        return remote(
            vsend.at[:, source_cols], tw.at[0, rows, cols],
            rim_send.at[side], rim_recv.at[side, source], device,
        )

    own_slots = slot_ids(ids_own)
    for c in range(IDROWS):
        slots[:, c * LANES : (c + 1) * LANES] = own_slots[c : c + 1, :]

    place = lax.broadcasted_iota(jnp.int32, (SLOTS, 1), 0)

    def place_own(pair):
        row = slots[:, 0:E_DEV] - pair * SLOTS
        onehot = jnp.where(row == place, 1.0, 0.0).astype(BF16)
        own = jnp.dot(onehot, blk[0:E_DEV, :], preferred_element_type=F32)
        cmat[pair] = own.astype(BF16)

    place_own(0)
    for n in range(nedges):

        @pl.when(x != n)
        def _(n=n):
            window(n, x).start()

        @pl.when(x == n)
        def _(n=n):
            first, last, at = windows[n]
            tw[0, own_rows, at : at + last - first] = vsend[:, first:last]

    own_rims = [rim(side, x) for side in range(2)]
    for copy in own_rims:
        copy.start()

    place_own(1)

    def halo(step, group, rows):
        return [
            remote(
                tw.at[step, rows, HALO + OWN - HALO : HALO + OWN], tw.at[step, rows, 0:HALO],
                halo_send.at[step, 0, group], halo_recv.at[step, 0, group], up,
            ),
            remote(
                tw.at[step, rows, HALO : 2 * HALO], tw.at[step, rows, HALO + OWN : WIDE],
                halo_send.at[step, 1, group], halo_recv.at[step, 1, group], down,
            ),
        ]

    group_rows = [slice(g * GROWS, (g + 1) * GROWS) for g in range(GROUPS)]
    halos = {}

    for copy in id_copies:
        copy.wait_recv()
    low_slots = slot_ids(ids_low)
    high_slots = slot_ids(ids_high)
    nends = ENDS // LANES
    for c in range(nends):
        low_row = slice(IDROWS - nends + c, IDROWS - nends + c + 1)
        high_row = slice(c, c + 1)
        at = E_DEV + c * LANES
        slots[:, at : at + LANES] = low_slots[low_row, :]
        at = at + ENDS
        slots[:, at : at + LANES] = high_slots[high_row, :]

    @pl.loop(0, PAIRS)
    def _(pair):
        row = slots[:, E_DEV : E_DEV + 2 * ENDS] - pair * SLOTS
        onehot_ends[pair] = jnp.where(row == place, 1.0, 0.0).astype(BF16)

    for copy in blk_copies:
        copy.wait_recv()

    lane = lax.broadcasted_iota(jnp.int32, (16, LANES), 1)
    upper = [(lane & (ORB << bit)) != 0 for bit in range(3)]
    for pair in range(PAIRS):
        ends = jnp.dot(
            onehot_ends[pair], fends[...], preferred_element_type=F32
        )
        placed = cmat[pair] + ends.astype(BF16)
        for k in range(NBAND):
            for side in range(2):
                cols = slice(side * LANES, (side + 1) * LANES)
                parts = []
                for i in range(TILE_ATOMS):
                    at = i * SLOTS_I + 16 * k
                    parts.append(placed[at : at + 16, cols])
                for bit in range(3):
                    width = ORB << bit
                    for n in range(8):
                        if n & (1 << bit):
                            continue
                        m = n | (1 << bit)
                        first = jnp.where(upper[bit], pltpu.roll(parts[m], width, 1), parts[n])
                        second = jnp.where(upper[bit], parts[m], pltpu.roll(parts[n], LANES - width, 1))
                        parts[n], parts[m] = first, second
                for n in range(8):
                    both = parts[n].astype(F32)
                    for s in range(2):
                        start = (pair * 2 * NBAND + 2 * k + s) * TILE + side * 8 + n
                        ht32[pl.ds(start, 8, stride=ORB), :] = both[8 * s : 8 * s + 8, :]
        ht[pair, NBAND * TILE : (NBAND + 1) * TILE, 0:TILE] = jnp.zeros((TILE, TILE), BF16)
        ht[pair, 0:TILE, TILE : 2 * TILE] = jnp.zeros((TILE, TILE), BF16)
        for a in range(2):
            t = 2 * pair + a
            piece = ht32[t * NBAND * TILE : (t + 1) * NBAND * TILE, :].astype(BF16)
            ht[pair, a * TILE : (a + NBAND) * TILE, a * TILE : (a + 1) * TILE] = piece

    def wait_windows(sources):
        for n in range(nedges):

            @pl.when(x == n)
            def _(n=n):
                for source in sources:
                    if source != n:
                        window(n, source).wait_recv()
                    if n == 0:
                        rim(0, source).wait_recv()
                    if n == nedges - 1:
                        rim(1, source).wait_recv()

    finals = []
    for step in range(1, STEPS + 1):
        for g in range(GROUPS):
            rows = group_rows[g]
            if step == 1:
                wait_windows(range(g * GROWS // own_vecs, (g + 1) * GROWS // own_vecs))
            else:
                for copy in halos[step - 1, g]:
                    copy.wait_recv()
            for pair in range(PAIRS):
                cols = slice(pair * 2 * TILE, (pair + 1) * 2 * TILE)
                wide = slice(pair * 2 * TILE, pair * 2 * TILE + (NBAND + 1) * TILE)
                product = jnp.dot(tw[step - 1, rows, wide], ht[pair], preferred_element_type=F32)
                mid = slice(HALO + pair * 2 * TILE, HALO + (pair + 1) * 2 * TILE)
                if step == 1:
                    new = product
                    total = coef_s[0] * tw[0, rows, mid].astype(F32) + coef_s[1] * new
                else:
                    if step == 2:
                        older = tw[0, rows, mid].astype(F32)
                    else:
                        older = tf[step - 3, rows, cols]
                    new = 2.0 * product - older
                    total = res[rows, cols] + coef_s[step] * new
                if step < STEPS:
                    tw[step, rows, mid] = new.astype(BF16)
                if step < STEPS - 1:
                    tf[step - 1, rows, cols] = new
                if step < STEPS:
                    res[rows, cols] = total
                else:
                    fsend = tw.at[STEPS]
                    fsend[rows, cols] = total.astype(BF16)
            if step < STEPS:
                halos[step, g] = halo(step, g, rows)
                for copy in halos[step, g]:
                    copy.start()
            else:
                for owner in range(g * GROWS // own_vecs, (g + 1) * GROWS // own_vecs):
                    vecs = slice(owner * own_vecs, (owner + 1) * own_vecs)
                    copy = remote(
                        tw.at[STEPS, vecs, 0:OWN], out.at[:, own_cols],
                        fin_send.at[owner], fin_recv.at[x], (r, owner),
                    )
                    finals.append(copy)

                    @pl.when(x != owner)
                    def _(copy=copy):
                        copy.start()

                    @pl.when(x == owner)
                    def _(vecs=vecs):
                        pltpu.make_async_copy(tw.at[STEPS, vecs, 0:OWN], out.at[:, own_cols], loc_sem.at[9]).start()

    for copy in id_copies + blk_copies + own_rims:
        copy.wait_send()
    for n in range(nedges):

        @pl.when(x != n)
        def _(n=n):
            window(n, x).wait_send()
    for pair in halos.values():
        for copy in pair:
            copy.wait_send()
    pltpu.make_async_copy(tw.at[STEPS, 0:own_vecs, 0:OWN], out.at[:, own_cols], loc_sem.at[9]).wait()
    for owner in range(nedges):

        @pl.when(x != owner)
        def _(owner=owner):
            finals[owner].wait_send()
            remote(
                tw.at[STEPS, 0:own_vecs, 0:OWN], out.at[:, owner * OWN : (owner + 1) * OWN],
                fin_send.at[owner], fin_recv.at[owner], (r, owner),
            ).wait_recv()


def per_device(nrows, nedges, features, edge_src, edge_dst, edge_cell, cell_bias, w_in, w_out, vectors, cheb_coef):
    ids = [a.reshape(IDROWS, LANES) for a in (edge_src, edge_dst, edge_cell)]
    own_vecs = VEC // nedges
    dma = pltpu.SemaphoreType.DMA
    anywhere = pl.BlockSpec(memory_space=pl.ANY)
    result = pl.pallas_call(
        functools.partial(kernel, nrows, nedges),
        out_shape=jax.ShapeDtypeStruct(vectors.shape, BF16),
        in_specs=[anywhere] * 9,
        out_specs=anywhere,
        scratch_shapes=[
            pltpu.VMEM((E_DEV, HID), BF16),
            pltpu.VMEM((2 * ENDS, HID), BF16),
            pltpu.VMEM((3, IDROWS, LANES), jnp.int32),
            pltpu.VMEM((2, IDROWS, LANES), jnp.int32),
            pltpu.VMEM((2, IDROWS, LANES), jnp.int32),
            pltpu.VMEM((3, 2 * HID), BF16),
            pltpu.SMEM((STEPS + 1,), F32),
            pltpu.VMEM((HID, 2 * HID), BF16),
            pltpu.VMEM((HID, HID), BF16),
            pltpu.VMEM((HID, HID), BF16),
            pltpu.VMEM(vectors.shape, F32),
            pltpu.VMEM(vectors.shape, BF16),
            pltpu.VMEM((1, E_DEV + 2 * ENDS), jnp.int32),
            pltpu.VMEM((E_DEV, LANES), F32),
            pltpu.VMEM((PAIRS, SLOTS, 2 * ENDS), BF16),
            pltpu.VMEM((E_DEV, HID), BF16),
            pltpu.VMEM((E_DEV, HID), BF16),
            pltpu.VMEM((PAIRS, SLOTS, HID), BF16),
            pltpu.VMEM((TROWS * NBAND * TILE, TILE), F32),
            pltpu.VMEM((PAIRS, (NBAND + 1) * TILE, 2 * TILE), BF16),
            pltpu.VMEM((STEPS + 1, VEC, WIDE), BF16),
            pltpu.VMEM((STEPS - 2, VEC, OWN), F32),
            pltpu.VMEM((VEC, OWN), F32),
            dma((10,)),
            dma((2, 2)),
            dma((2, 2)),
            dma((2,)),
            dma((2,)),
            dma((nedges,)),
            dma((nedges,)),
            dma((2,)),
            dma((2, nedges)),
            dma((STEPS, 2, GROUPS)),
            dma((STEPS, 2, GROUPS)),
            dma((nedges,)),
            dma((nedges,)),
        ],
        compiler_params=pltpu.CompilerParams(
            collective_id=0, has_side_effects=True
        ),
        name="filter",
    )(features, *ids, cell_bias, w_in, w_out, vectors, cheb_coef)
    return result.astype(F32)


def solution(mesh):
    nrows, nedges = mesh.shape["rows"], mesh.shape["edges"]
    placed = (
        P(("rows", "edges"), None),
        P(("rows", "edges")),
        P(("rows", "edges")),
        P(("rows", "edges")),
        P(),
        P(),
        P(),
        P("edges", "rows"),
        P(),
    )
    return jax.shard_map(
        functools.partial(per_device, nrows, nedges),
        mesh=mesh,
        in_specs=placed,
        out_specs=P("edges", "rows"),
        check_vma=False,
    )
```

```python
import functools

import jax
import jax.numpy as jnp
from jax import lax
from jax.experimental import pallas as pl
from jax.experimental.pallas import tpu as pltpu
from jax.sharding import PartitionSpec as P

MESH = pl.DeviceIdType.MESH
BF16 = jnp.bfloat16
F32 = jnp.float32

ORB = 16
TILE_ATOMS = 8
BAND = 3
NBAND = 2 * BAND + 1
HID = 256
VEC = 128
STEPS = 4
ATOM_Q = 32
SPILL = 320
E_DEV = 1280
TILE = TILE_ATOMS * ORB
TROWS = ATOM_Q // TILE_ATOMS
OWN = TROWS * TILE
HALO = BAND * TILE
WIDE = OWN + 2 * HALO
LANES = 128
IDROWS = E_DEV // LANES
PAIRS = TROWS // 2
SLOTS_I = 2 * NBAND * TILE_ATOMS
SLOTS = TILE_ATOMS * SLOTS_I
ENDS = 384
PAD = ENDS - SPILL
GROUPS = 2
GROWS = VEC // GROUPS


def kernel(
    nrows, nedges,
    feat, src, dst, cell, bias, w_in, w_out, vec, coef,
    out,
    fown, fends, ids_own, ids_low, ids_high, bias_v, coef_s, win_v, wout_v, wperm, vec_v, vsend,
    slots, cells, onehot_ends, hid, blk, cmat, ht32, ht, tw, tf, res,
    loc_sem, ids_send, ids_recv, feat_send, feat_recv, win_send, win_recv, rim_send, rim_recv,
    halo_send, halo_recv, fin_send, fin_recv,
):
    r = lax.axis_index("rows")
    x = lax.axis_index("edges")
    quarter = r * nedges + x
    ntiles = nrows * nedges * TROWS
    own_vecs = VEC // nedges

    up_x = lax.rem(x + 1, nedges)
    up_r = lax.rem(r + (x + 1) // nedges, nrows)
    down_x = lax.rem(x + nedges - 1, nedges)
    down_r = lax.rem(r + nrows - 1 + (x + nedges - 1) // nedges, nrows)
    up = (up_r, up_x)
    down = (down_r, down_x)

    def remote(source, target, send, recv, device):
        return pltpu.make_async_remote_copy(
            src_ref=source, dst_ref=target, send_sem=send, recv_sem=recv,
            device_id=device, device_id_type=MESH,
        )

    loads = [
        pltpu.make_async_copy(vec, vec_v, loc_sem.at[0]),
        pltpu.make_async_copy(w_out, wout_v, loc_sem.at[1]),
        pltpu.make_async_copy(w_in, win_v, loc_sem.at[2]),
        pltpu.make_async_copy(bias, bias_v, loc_sem.at[3]),
        pltpu.make_async_copy(feat, fown, loc_sem.at[4]),
        pltpu.make_async_copy(src, ids_own.at[0], loc_sem.at[5]),
        pltpu.make_async_copy(dst, ids_own.at[1], loc_sem.at[6]),
        pltpu.make_async_copy(cell, ids_own.at[2], loc_sem.at[7]),
        pltpu.make_async_copy(coef, coef_s, loc_sem.at[8]),
    ]
    barrier = pltpu.get_barrier_semaphore()
    after_r = lax.rem(r + 1, nrows)
    before_r = lax.rem(r + nrows - 1, nrows)

    def greet(device):
        pl.semaphore_signal(barrier, inc=1, device_id=device, device_id_type=MESH)

    for device in [up, down] + [(r, lax.rem(x + off, nedges)) for off in range(1, nedges)]:
        greet(device)

    @pl.when(x == 0)
    def _():
        for n in range(nedges):
            greet((before_r, n))

    @pl.when(x == nedges - 1)
    def _():
        for n in range(nedges):
            greet((after_r, n))

    for load in loads:
        load.start()

    loads[1].wait()
    k_id = lax.broadcasted_iota(jnp.int32, (HID, HID), 0)
    n_id = lax.broadcasted_iota(jnp.int32, (HID, HID), 1)
    swap = jnp.logical_and(n_id // ORB == k_id % ORB, n_id % ORB == k_id // ORB)
    perm = jnp.where(swap, 1.0, 0.0).astype(BF16)
    wperm[...] = jnp.dot(wout_v[...], perm, preferred_element_type=F32).astype(BF16)
    for load in loads[2:]:
        load.wait()
    half = jnp.where(lax.broadcasted_iota(jnp.int32, (1, 2 * HID), 1) < HID, 0.5, 1.0)
    win_v[...] = (win_v[...].astype(F32) * half).astype(BF16)
    bias_of = [bias_v[n : n + 1, :].astype(F32) * half for n in range(3)]

    def pair_net(at, count):
        for n in range(at, at + count, LANES):
            row = ids_own[2, n // LANES : n // LANES + 1, :]
            cells[n : n + LANES, :] = jnp.broadcast_to(row.astype(F32), (LANES, LANES)).T
        for first in range(at, at + count, 128):
            rows = slice(first, first + 128)
            kind = cells[rows, :]
            second, third = kind > 0.5, kind > 1.5
            pre = jnp.dot(fown[rows, :], win_v[...], preferred_element_type=F32)
            parts = []
            for c in range(0, 2 * HID, LANES):
                b0, b1, b2 = [b[:, c : c + LANES] for b in bias_of]
                parts.append(pre[:, c : c + LANES] + jnp.where(third, b2, jnp.where(second, b1, b0)))
            for n in range(HID // LANES):
                gate = parts[n]
                value = (gate + gate * jnp.tanh(gate)) * parts[n + HID // LANES]
                hid[rows, n * LANES : (n + 1) * LANES] = value.astype(BF16)
        rows = slice(at, at + count)
        blk[rows, :] = jnp.dot(hid[rows, :], wperm[...], preferred_element_type=F32).astype(BF16)

    def slot_ids(ids):
        source = ids[0]
        goal = ids[1]
        local = source % ATOM_Q
        shift = goal // TILE_ATOMS - source // TILE_ATOMS + BAND
        shift = jnp.where(shift < 0, shift + ntiles, shift)
        shift = jnp.where(shift >= ntiles, shift - ntiles, shift)
        tile = local // TILE_ATOMS
        slot = (
            tile // 2 * SLOTS
            + (local % TILE_ATOMS) * SLOTS_I
            + (tile % 2 * NBAND + shift) * TILE_ATOMS
            + goal % TILE_ATOMS
        )
        return jnp.where(source // ATOM_Q == quarter, slot, -1)

    ends_rows = (slice(0, ENDS), slice(E_DEV - ENDS, E_DEV))
    for rows in ends_rows:
        pair_net(rows.start, ENDS)

    loads[0].wait()
    vsend[...] = vec_v[...].astype(BF16)
    own_cols = pl.ds(pl.multiple_of(x * OWN, OWN), OWN)
    own_rows = pl.ds(pl.multiple_of(x * own_vecs, own_vecs), own_vecs)
    fends[0:PAD, :] = jnp.zeros((PAD, HID), BF16)
    fends[2 * ENDS - PAD : 2 * ENDS, :] = jnp.zeros((PAD, HID), BF16)

    pl.semaphore_wait(barrier, nedges + 3)

    id_copies = []
    for n, ref in enumerate((src, dst)):
        id_copies.append(remote(ref, ids_low.at[n], ids_send.at[0, n], ids_recv.at[0, n], up))
        id_copies.append(remote(ref, ids_high.at[n], ids_send.at[1, n], ids_recv.at[1, n], down))
    blk_copies = [
        remote(blk.at[E_DEV - SPILL : E_DEV], fends.at[PAD:ENDS], feat_send.at[0], feat_recv.at[0], up),
        remote(blk.at[0:SPILL], fends.at[ENDS : ENDS + SPILL], feat_send.at[1], feat_recv.at[1], down),
    ]
    for copy in id_copies + blk_copies:
        copy.start()
    pair_net(ENDS, E_DEV - 2 * ENDS)

    windows = []
    for n in range(nedges):
        first = max(n * OWN - HALO, 0)
        last = min((n + 1) * OWN + HALO, nedges * OWN)
        at = first - (n * OWN - HALO)
        windows.append((first, last, at))

    def window(n, source):
        first, last, at = windows[n]
        rows = pl.ds(pl.multiple_of(source * own_vecs, own_vecs), own_vecs)
        return remote(
            vsend.at[:, first:last], tw.at[0, rows, at : at + last - first],
            win_send.at[n], win_recv.at[source], (r, n),
        )

    def rim(side, source):
        rows = pl.ds(pl.multiple_of(source * own_vecs, own_vecs), own_vecs)
        if side == 0:
            source_cols, cols, device = slice(nedges * OWN - HALO, nedges * OWN), slice(0, HALO), (after_r, 0)
        else:
            source_cols, cols, device = slice(0, HALO), slice(HALO + OWN, WIDE), (before_r, nedges - 1)
        return remote(
            vsend.at[:, source_cols], tw.at[0, rows, cols],
            rim_send.at[side], rim_recv.at[side, source], device,
        )

    own_slots = slot_ids(ids_own)
    for c in range(IDROWS):
        slots[:, c * LANES : (c + 1) * LANES] = own_slots[c : c + 1, :]

    place = lax.broadcasted_iota(jnp.int32, (SLOTS, 1), 0)

    def place_own(pair):
        row = slots[:, 0:E_DEV] - pair * SLOTS
        onehot = jnp.where(row == place, 1.0, 0.0).astype(BF16)
        own = jnp.dot(onehot, blk[0:E_DEV, :], preferred_element_type=F32)
        cmat[pair] = own.astype(BF16)

    place_own(0)
    for n in range(nedges):

        @pl.when(x != n)
        def _(n=n):
            window(n, x).start()

        @pl.when(x == n)
        def _(n=n):
            first, last, at = windows[n]
            tw[0, own_rows, at : at + last - first] = vsend[:, first:last]

    own_rims = [rim(side, x) for side in range(2)]
    for copy in own_rims:
        copy.start()

    place_own(1)

    def halo(step, group, rows):
        return [
            remote(
                tw.at[step, rows, HALO + OWN - HALO : HALO + OWN], tw.at[step, rows, 0:HALO],
                halo_send.at[step, 0, group], halo_recv.at[step, 0, group], up,
            ),
            remote(
                tw.at[step, rows, HALO : 2 * HALO], tw.at[step, rows, HALO + OWN : WIDE],
                halo_send.at[step, 1, group], halo_recv.at[step, 1, group], down,
            ),
        ]

    group_rows = [slice(g * GROWS, (g + 1) * GROWS) for g in range(GROUPS)]
    halos = {}

    for copy in id_copies:
        copy.wait_recv()
    low_slots = slot_ids(ids_low)
    high_slots = slot_ids(ids_high)
    nends = ENDS // LANES
    for c in range(nends):
        low_row = slice(IDROWS - nends + c, IDROWS - nends + c + 1)
        high_row = slice(c, c + 1)
        at = E_DEV + c * LANES
        slots[:, at : at + LANES] = low_slots[low_row, :]
        at = at + ENDS
        slots[:, at : at + LANES] = high_slots[high_row, :]

    @pl.loop(0, PAIRS)
    def _(pair):
        row = slots[:, E_DEV : E_DEV + 2 * ENDS] - pair * SLOTS
        onehot_ends[pair] = jnp.where(row == place, 1.0, 0.0).astype(BF16)

    for copy in blk_copies:
        copy.wait_recv()

    group = lax.broadcasted_iota(jnp.int32, (16, LANES), 1)
    odd = [(group & (ORB << bit)) != 0 for bit in range(3)]
    for pair in range(PAIRS):
        for a in range(2):
            t = 2 * pair + a
            free = 0 if a else NBAND * TILE
            ht[t, free : free + TILE, :] = jnp.zeros((TILE, TILE), BF16)
        ends = jnp.dot(onehot_ends[pair], fends[...], preferred_element_type=F32)
        cmat[pair] = cmat[pair] + ends.astype(BF16)
        for k in range(NBAND):
            for side in range(2):
                cols = slice(side * LANES, (side + 1) * LANES)
                parts = []
                for i in range(TILE_ATOMS):
                    at = i * SLOTS_I + 16 * k
                    part = cmat[pair, at : at + 16, cols]
                    parts.append(pltpu.roll(part, i * ORB, 1) if i else part)
                for q in range(8):
                    level = [parts[(g - q) % 8] for g in range(8)]
                    for bit in range(3):
                        level = [
                            jnp.where(odd[bit], level[n + 1], level[n])
                            for n in range(0, len(level), 2)
                        ]
                    both = pltpu.roll(level[0], LANES - q * ORB, 1) if q else level[0]
                    both = both.astype(F32)
                    for s in range(2):
                        start = (pair * 2 * NBAND + 2 * k + s) * TILE + (side * 8 + q) * TILE_ATOMS
                        ht32[start : start + TILE_ATOMS, :] = both[8 * s : 8 * s + 8, :]
            for s in range(2):
                a, d = divmod(2 * k + s, NBAND)
                for j in range(TILE_ATOMS):
                    start = (pair * 2 * NBAND + 2 * k + s) * TILE + j
                    piece = ht32[pl.ds(start, ORB, stride=TILE_ATOMS), :].astype(BF16)
                    at = (a + d) * TILE + j * ORB
                    ht[2 * pair + a, at : at + ORB, :] = piece

    def wait_windows(sources):
        for n in range(nedges):

            @pl.when(x == n)
            def _(n=n):
                for source in sources:
                    if source != n:
                        window(n, source).wait_recv()
                    if n == 0:
                        rim(0, source).wait_recv()
                    if n == nedges - 1:
                        rim(1, source).wait_recv()

    finals = []
    for step in range(1, STEPS + 1):
        for g in range(GROUPS):
            rows = group_rows[g]
            if step == 1:
                wait_windows(range(g * GROWS // own_vecs, (g + 1) * GROWS // own_vecs))
            else:
                for copy in halos[step - 1, g]:
                    copy.wait_recv()
            for pair in range(PAIRS):
                cols = slice(pair * 2 * TILE, (pair + 1) * 2 * TILE)
                wide = slice(pair * 2 * TILE, pair * 2 * TILE + (NBAND + 1) * TILE)
                band = jnp.concatenate([ht[2 * pair], ht[2 * pair + 1]], axis=1)
                product = jnp.dot(tw[step - 1, rows, wide], band, preferred_element_type=F32)
                mid = slice(HALO + pair * 2 * TILE, HALO + (pair + 1) * 2 * TILE)
                if step == 1:
                    new = product
                    total = coef_s[0] * tw[0, rows, mid].astype(F32) + coef_s[1] * new
                else:
                    if step == 2:
                        older = tw[0, rows, mid].astype(F32)
                    else:
                        older = tf[step - 3, rows, cols]
                    new = 2.0 * product - older
                    total = res[rows, cols] + coef_s[step] * new
                if step < STEPS:
                    tw[step, rows, mid] = new.astype(BF16)
                if step < STEPS - 1:
                    tf[step - 1, rows, cols] = new
                if step < STEPS:
                    res[rows, cols] = total
                else:
                    fsend = tw.at[STEPS]
                    fsend[rows, cols] = total.astype(BF16)
            if step < STEPS:
                halos[step, g] = halo(step, g, rows)
                for copy in halos[step, g]:
                    copy.start()
            else:
                for owner in range(g * GROWS // own_vecs, (g + 1) * GROWS // own_vecs):
                    vecs = slice(owner * own_vecs, (owner + 1) * own_vecs)
                    copy = remote(
                        tw.at[STEPS, vecs, 0:OWN], out.at[:, own_cols],
                        fin_send.at[owner], fin_recv.at[x], (r, owner),
                    )
                    finals.append(copy)

                    @pl.when(x != owner)
                    def _(copy=copy):
                        copy.start()

                    @pl.when(x == owner)
                    def _(vecs=vecs):
                        pltpu.make_async_copy(tw.at[STEPS, vecs, 0:OWN], out.at[:, own_cols], loc_sem.at[9]).start()

    for copy in id_copies + blk_copies + own_rims:
        copy.wait_send()
    for n in range(nedges):

        @pl.when(x != n)
        def _(n=n):
            window(n, x).wait_send()
    for pair in halos.values():
        for copy in pair:
            copy.wait_send()
    pltpu.make_async_copy(tw.at[STEPS, 0:own_vecs, 0:OWN], out.at[:, own_cols], loc_sem.at[9]).wait()
    for owner in range(nedges):

        @pl.when(x != owner)
        def _(owner=owner):
            finals[owner].wait_send()
            remote(
                tw.at[STEPS, 0:own_vecs, 0:OWN], out.at[:, owner * OWN : (owner + 1) * OWN],
                fin_send.at[owner], fin_recv.at[owner], (r, owner),
            ).wait_recv()


def per_device(nrows, nedges, features, edge_src, edge_dst, edge_cell, cell_bias, w_in, w_out, vectors, cheb_coef):
    ids = [a.reshape(IDROWS, LANES) for a in (edge_src, edge_dst, edge_cell)]
    own_vecs = VEC // nedges
    dma = pltpu.SemaphoreType.DMA
    anywhere = pl.BlockSpec(memory_space=pl.ANY)
    result = pl.pallas_call(
        functools.partial(kernel, nrows, nedges),
        out_shape=jax.ShapeDtypeStruct(vectors.shape, BF16),
        in_specs=[anywhere] * 9,
        out_specs=anywhere,
        scratch_shapes=[
            pltpu.VMEM((E_DEV, HID), BF16),
            pltpu.VMEM((2 * ENDS, HID), BF16),
            pltpu.VMEM((3, IDROWS, LANES), jnp.int32),
            pltpu.VMEM((2, IDROWS, LANES), jnp.int32),
            pltpu.VMEM((2, IDROWS, LANES), jnp.int32),
            pltpu.VMEM((3, 2 * HID), BF16),
            pltpu.SMEM((STEPS + 1,), F32),
            pltpu.VMEM((HID, 2 * HID), BF16),
            pltpu.VMEM((HID, HID), BF16),
            pltpu.VMEM((HID, HID), BF16),
            pltpu.VMEM(vectors.shape, F32),
            pltpu.VMEM(vectors.shape, BF16),
            pltpu.VMEM((1, E_DEV + 2 * ENDS), jnp.int32),
            pltpu.VMEM((E_DEV, LANES), F32),
            pltpu.VMEM((PAIRS, SLOTS, 2 * ENDS), BF16),
            pltpu.VMEM((E_DEV, HID), BF16),
            pltpu.VMEM((E_DEV, HID), BF16),
            pltpu.VMEM((PAIRS, SLOTS, HID), BF16),
            pltpu.VMEM((TROWS * NBAND * TILE, TILE), F32),
            pltpu.VMEM((TROWS, (NBAND + 1) * TILE, TILE), BF16),
            pltpu.VMEM((STEPS + 1, VEC, WIDE), BF16),
            pltpu.VMEM((STEPS - 2, VEC, OWN), F32),
            pltpu.VMEM((VEC, OWN), F32),
            dma((10,)),
            dma((2, 2)),
            dma((2, 2)),
            dma((2,)),
            dma((2,)),
            dma((nedges,)),
            dma((nedges,)),
            dma((2,)),
            dma((2, nedges)),
            dma((STEPS, 2, GROUPS)),
            dma((STEPS, 2, GROUPS)),
            dma((nedges,)),
            dma((nedges,)),
        ],
        compiler_params=pltpu.CompilerParams(
            collective_id=0, has_side_effects=True
        ),
        name="filter",
    )(features, *ids, cell_bias, w_in, w_out, vectors, cheb_coef)
    return result.astype(F32)


def solution(mesh):
    nrows, nedges = mesh.shape["rows"], mesh.shape["edges"]
    placed = (
        P(("rows", "edges"), None),
        P(("rows", "edges")),
        P(("rows", "edges")),
        P(("rows", "edges")),
        P(),
        P(),
        P(),
        P("edges", "rows"),
        P(),
    )
    return jax.shard_map(
        functools.partial(per_device, nrows, nedges),
        mesh=mesh,
        in_specs=placed,
        out_specs=P("edges", "rows"),
        check_vma=False,
    )
```

```python
import functools

import jax
import jax.numpy as jnp
from jax import lax
from jax.experimental import pallas as pl
from jax.experimental.pallas import tpu as pltpu
from jax.sharding import PartitionSpec as P

MESH = pl.DeviceIdType.MESH
BF16 = jnp.bfloat16
F32 = jnp.float32

ORB = 16
TILE_ATOMS = 8
BAND = 3
NBAND = 2 * BAND + 1
HID = 256
VEC = 128
STEPS = 4
ATOM_Q = 32
SPILL = 320
E_DEV = 1280
TILE = TILE_ATOMS * ORB
TROWS = ATOM_Q // TILE_ATOMS
OWN = TROWS * TILE
HALO = BAND * TILE
WIDE = OWN + 2 * HALO
LANES = 128
IDROWS = E_DEV // LANES
PAIRS = TROWS // 2
SLOTS_I = 2 * NBAND * TILE_ATOMS
SLOTS = TILE_ATOMS * SLOTS_I
ENDS = 384
PAD = ENDS - SPILL
GROUPS = 4
GROWS = VEC // GROUPS


def kernel(
    nrows, nedges,
    feat, src, dst, cell, bias, w_in, w_out, vec, coef,
    out,
    fown, fends, ids_own, ids_low, ids_high, bias_v, coef_s, win_v, wout_v, wperm, vec_v, vsend,
    slots, cells, onehot_ends, hid, blk, cmat, ht32, ht, tw, tf, res,
    loc_sem, ids_send, ids_recv, feat_send, feat_recv, win_send, win_recv, rim_send, rim_recv,
    halo_send, halo_recv, fin_send, fin_recv,
):
    r = lax.axis_index("rows")
    x = lax.axis_index("edges")
    quarter = r * nedges + x
    ntiles = nrows * nedges * TROWS
    own_vecs = VEC // nedges

    up_x = lax.rem(x + 1, nedges)
    up_r = lax.rem(r + (x + 1) // nedges, nrows)
    down_x = lax.rem(x + nedges - 1, nedges)
    down_r = lax.rem(r + nrows - 1 + (x + nedges - 1) // nedges, nrows)
    up = (up_r, up_x)
    down = (down_r, down_x)

    def remote(source, target, send, recv, device):
        return pltpu.make_async_remote_copy(
            src_ref=source, dst_ref=target, send_sem=send, recv_sem=recv,
            device_id=device, device_id_type=MESH,
        )

    loads = [
        pltpu.make_async_copy(vec, vec_v, loc_sem.at[0]),
        pltpu.make_async_copy(w_out, wout_v, loc_sem.at[1]),
        pltpu.make_async_copy(w_in, win_v, loc_sem.at[2]),
        pltpu.make_async_copy(bias, bias_v, loc_sem.at[3]),
        pltpu.make_async_copy(feat, fown, loc_sem.at[4]),
        pltpu.make_async_copy(src, ids_own.at[0], loc_sem.at[5]),
        pltpu.make_async_copy(dst, ids_own.at[1], loc_sem.at[6]),
        pltpu.make_async_copy(cell, ids_own.at[2], loc_sem.at[7]),
        pltpu.make_async_copy(coef, coef_s, loc_sem.at[8]),
    ]
    barrier = pltpu.get_barrier_semaphore()
    after_r = lax.rem(r + 1, nrows)
    before_r = lax.rem(r + nrows - 1, nrows)

    def greet(device):
        pl.semaphore_signal(barrier, inc=1, device_id=device, device_id_type=MESH)

    for device in [up, down] + [(r, lax.rem(x + off, nedges)) for off in range(1, nedges)]:
        greet(device)

    @pl.when(x == 0)
    def _():
        for n in range(nedges):
            greet((before_r, n))

    @pl.when(x == nedges - 1)
    def _():
        for n in range(nedges):
            greet((after_r, n))

    for load in loads:
        load.start()

    loads[1].wait()
    k_id = lax.broadcasted_iota(jnp.int32, (HID, HID), 0)
    n_id = lax.broadcasted_iota(jnp.int32, (HID, HID), 1)
    swap = jnp.logical_and(n_id // ORB == k_id % ORB, n_id % ORB == k_id // ORB)
    perm = jnp.where(swap, 1.0, 0.0).astype(BF16)
    wperm[...] = jnp.dot(wout_v[...], perm, preferred_element_type=F32).astype(BF16)
    for load in loads[2:]:
        load.wait()
    half = jnp.where(lax.broadcasted_iota(jnp.int32, (1, 2 * HID), 1) < HID, 0.5, 1.0)
    win_v[...] = (win_v[...].astype(F32) * half).astype(BF16)
    bias_of = [bias_v[n : n + 1, :].astype(F32) * half for n in range(3)]

    def pair_net(at, count):
        for n in range(at, at + count, LANES):
            row = ids_own[2, n // LANES : n // LANES + 1, :]
            cells[n : n + LANES, :] = jnp.broadcast_to(row.astype(F32), (LANES, LANES)).T
        for first in range(at, at + count, 128):
            rows = slice(first, first + 128)
            kind = cells[rows, :]
            second, third = kind > 0.5, kind > 1.5
            pre = jnp.dot(fown[rows, :], win_v[...], preferred_element_type=F32)
            parts = []
            for c in range(0, 2 * HID, LANES):
                b0, b1, b2 = [b[:, c : c + LANES] for b in bias_of]
                parts.append(pre[:, c : c + LANES] + jnp.where(third, b2, jnp.where(second, b1, b0)))
            for n in range(HID // LANES):
                gate = parts[n]
                value = (gate + gate * jnp.tanh(gate)) * parts[n + HID // LANES]
                hid[rows, n * LANES : (n + 1) * LANES] = value.astype(BF16)
        rows = slice(at, at + count)
        blk[rows, :] = jnp.dot(hid[rows, :], wperm[...], preferred_element_type=F32).astype(BF16)

    def slot_ids(ids):
        source = ids[0]
        goal = ids[1]
        local = source % ATOM_Q
        shift = goal // TILE_ATOMS - source // TILE_ATOMS + BAND
        shift = jnp.where(shift < 0, shift + ntiles, shift)
        shift = jnp.where(shift >= ntiles, shift - ntiles, shift)
        tile = local // TILE_ATOMS
        slot = (
            tile // 2 * SLOTS
            + (local % TILE_ATOMS) * SLOTS_I
            + (tile % 2 * NBAND + shift) * TILE_ATOMS
            + goal % TILE_ATOMS
        )
        return jnp.where(source // ATOM_Q == quarter, slot, -1)

    ends_rows = (slice(0, ENDS), slice(E_DEV - ENDS, E_DEV))
    for rows in ends_rows:
        pair_net(rows.start, ENDS)

    loads[0].wait()
    vsend[...] = vec_v[...].astype(BF16)
    own_cols = pl.ds(pl.multiple_of(x * OWN, OWN), OWN)
    own_rows = pl.ds(pl.multiple_of(x * own_vecs, own_vecs), own_vecs)
    fends[0:PAD, :] = jnp.zeros((PAD, HID), BF16)
    fends[2 * ENDS - PAD : 2 * ENDS, :] = jnp.zeros((PAD, HID), BF16)

    pl.semaphore_wait(barrier, nedges + 3)

    id_copies = []
    for n, ref in enumerate((src, dst)):
        id_copies.append(remote(ref, ids_low.at[n], ids_send.at[0, n], ids_recv.at[0, n], up))
        id_copies.append(remote(ref, ids_high.at[n], ids_send.at[1, n], ids_recv.at[1, n], down))
    blk_copies = [
        remote(blk.at[E_DEV - SPILL : E_DEV], fends.at[PAD:ENDS], feat_send.at[0], feat_recv.at[0], up),
        remote(blk.at[0:SPILL], fends.at[ENDS : ENDS + SPILL], feat_send.at[1], feat_recv.at[1], down),
    ]
    for copy in id_copies + blk_copies:
        copy.start()
    pair_net(ENDS, E_DEV - 2 * ENDS)

    windows = []
    for n in range(nedges):
        first = max(n * OWN - HALO, 0)
        last = min((n + 1) * OWN + HALO, nedges * OWN)
        at = first - (n * OWN - HALO)
        windows.append((first, last, at))

    def window(n, source):
        first, last, at = windows[n]
        rows = pl.ds(pl.multiple_of(source * own_vecs, own_vecs), own_vecs)
        return remote(
            vsend.at[:, first:last], tw.at[0, rows, at : at + last - first],
            win_send.at[n], win_recv.at[source], (r, n),
        )

    def rim(side, source):
        rows = pl.ds(pl.multiple_of(source * own_vecs, own_vecs), own_vecs)
        if side == 0:
            source_cols, cols, device = slice(nedges * OWN - HALO, nedges * OWN), slice(0, HALO), (after_r, 0)
        else:
            source_cols, cols, device = slice(0, HALO), slice(HALO + OWN, WIDE), (before_r, nedges - 1)
        return remote(
            vsend.at[:, source_cols], tw.at[0, rows, cols],
            rim_send.at[side], rim_recv.at[side, source], device,
        )

    own_slots = slot_ids(ids_own)
    for c in range(IDROWS):
        slots[:, c * LANES : (c + 1) * LANES] = own_slots[c : c + 1, :]

    place = lax.broadcasted_iota(jnp.int32, (SLOTS, 1), 0)

    def place_own(pair):
        row = slots[:, 0:E_DEV] - pair * SLOTS
        onehot = jnp.where(row == place, 1.0, 0.0).astype(BF16)
        own = jnp.dot(onehot, blk[0:E_DEV, :], preferred_element_type=F32)
        cmat[pair] = own.astype(BF16)

    place_own(0)
    for n in range(nedges):

        @pl.when(x != n)
        def _(n=n):
            window(n, x).start()

        @pl.when(x == n)
        def _(n=n):
            first, last, at = windows[n]
            tw[0, own_rows, at : at + last - first] = vsend[:, first:last]

    own_rims = [rim(side, x) for side in range(2)]
    for copy in own_rims:
        copy.start()

    place_own(1)

    def halo(step, group, rows):
        return [
            remote(
                tw.at[step, rows, HALO + OWN - HALO : HALO + OWN], tw.at[step, rows, 0:HALO],
                halo_send.at[step, 0, group], halo_recv.at[step, 0, group], up,
            ),
            remote(
                tw.at[step, rows, HALO : 2 * HALO], tw.at[step, rows, HALO + OWN : WIDE],
                halo_send.at[step, 1, group], halo_recv.at[step, 1, group], down,
            ),
        ]

    group_rows = [slice(g * GROWS, (g + 1) * GROWS) for g in range(GROUPS)]
    halos = {}

    for copy in id_copies:
        copy.wait_recv()
    low_slots = slot_ids(ids_low)
    high_slots = slot_ids(ids_high)
    nends = ENDS // LANES
    for c in range(nends):
        low_row = slice(IDROWS - nends + c, IDROWS - nends + c + 1)
        high_row = slice(c, c + 1)
        at = E_DEV + c * LANES
        slots[:, at : at + LANES] = low_slots[low_row, :]
        at = at + ENDS
        slots[:, at : at + LANES] = high_slots[high_row, :]

    @pl.loop(0, PAIRS)
    def _(pair):
        row = slots[:, E_DEV : E_DEV + 2 * ENDS] - pair * SLOTS
        onehot_ends[pair] = jnp.where(row == place, 1.0, 0.0).astype(BF16)

    for t in range(TROWS):
        free = 0 if t % 2 else NBAND * TILE
        ht[t, free : free + TILE, :] = jnp.zeros((TILE, TILE), BF16)
    for copy in blk_copies:
        copy.wait_recv()

    group = lax.broadcasted_iota(jnp.int32, (16, LANES), 1)
    odd = [(group & (ORB << bit)) != 0 for bit in range(3)]
    for pair in range(PAIRS):
        ends = jnp.dot(onehot_ends[pair], fends[...], preferred_element_type=F32)
        cmat[pair] = cmat[pair] + ends.astype(BF16)
    for pair in range(PAIRS):
        for k in range(NBAND):
            for side in range(2):
                cols = slice(side * LANES, (side + 1) * LANES)
                parts = []
                for i in range(TILE_ATOMS):
                    at = i * SLOTS_I + 16 * k
                    part = cmat[pair, at : at + 16, cols]
                    parts.append(pltpu.roll(part, i * ORB, 1) if i else part)
                for q in range(8):
                    level = [parts[(g - q) % 8] for g in range(8)]
                    for bit in range(3):
                        level = [
                            jnp.where(odd[bit], level[n + 1], level[n])
                            for n in range(0, len(level), 2)
                        ]
                    both = pltpu.roll(level[0], LANES - q * ORB, 1) if q else level[0]
                    both = both.astype(F32)
                    for s in range(2):
                        start = (pair * 2 * NBAND + 2 * k + s) * TILE + (side * 8 + q) * TILE_ATOMS
                        ht32[start : start + TILE_ATOMS, :] = both[8 * s : 8 * s + 8, :]
            for s in range(2):
                a, d = divmod(2 * k + s, NBAND)
                for j in range(TILE_ATOMS):
                    start = (pair * 2 * NBAND + 2 * k + s) * TILE + j
                    piece = ht32[pl.ds(start, ORB, stride=TILE_ATOMS), :].astype(BF16)
                    at = (a + d) * TILE + j * ORB
                    ht[2 * pair + a, at : at + ORB, :] = piece

    def wait_windows(sources):
        for n in range(nedges):

            @pl.when(x == n)
            def _(n=n):
                for source in sources:
                    if source != n:
                        window(n, source).wait_recv()
                    if n == 0:
                        rim(0, source).wait_recv()
                    if n == nedges - 1:
                        rim(1, source).wait_recv()

    finals = []
    for step in range(1, STEPS + 1):
        for g in range(GROUPS):
            rows = group_rows[g]
            if step == 1:
                wait_windows(range(g * GROWS // own_vecs, (g + 1) * GROWS // own_vecs))
            else:
                for copy in halos[step - 1, g]:
                    copy.wait_recv()
            for pair in range(PAIRS):
                cols = slice(pair * 2 * TILE, (pair + 1) * 2 * TILE)
                wide = slice(pair * 2 * TILE, pair * 2 * TILE + (NBAND + 1) * TILE)
                band = jnp.concatenate([ht[2 * pair], ht[2 * pair + 1]], axis=1)
                product = jnp.dot(tw[step - 1, rows, wide], band, preferred_element_type=F32)
                mid = slice(HALO + pair * 2 * TILE, HALO + (pair + 1) * 2 * TILE)
                if step == 1:
                    new = product
                    total = coef_s[0] * tw[0, rows, mid].astype(F32) + coef_s[1] * new
                else:
                    if step == 2:
                        older = tw[0, rows, mid].astype(F32)
                    else:
                        older = tf[step - 3, rows, cols]
                    new = 2.0 * product - older
                    total = res[rows, cols] + coef_s[step] * new
                if step < STEPS:
                    tw[step, rows, mid] = new.astype(BF16)
                if step < STEPS - 1:
                    tf[step - 1, rows, cols] = new
                if step < STEPS:
                    res[rows, cols] = total
                else:
                    fsend = tw.at[STEPS]
                    fsend[rows, cols] = total.astype(BF16)
            if step < STEPS:
                halos[step, g] = halo(step, g, rows)
                for copy in halos[step, g]:
                    copy.start()
            else:
                for owner in range(g * GROWS // own_vecs, (g + 1) * GROWS // own_vecs):
                    vecs = slice(owner * own_vecs, (owner + 1) * own_vecs)
                    copy = remote(
                        tw.at[STEPS, vecs, 0:OWN], out.at[:, own_cols],
                        fin_send.at[owner], fin_recv.at[x], (r, owner),
                    )
                    finals.append(copy)

                    @pl.when(x != owner)
                    def _(copy=copy):
                        copy.start()

                    @pl.when(x == owner)
                    def _(vecs=vecs):
                        pltpu.make_async_copy(tw.at[STEPS, vecs, 0:OWN], out.at[:, own_cols], loc_sem.at[9]).start()

    for copy in id_copies + blk_copies + own_rims:
        copy.wait_send()
    for n in range(nedges):

        @pl.when(x != n)
        def _(n=n):
            window(n, x).wait_send()
    for pair in halos.values():
        for copy in pair:
            copy.wait_send()
    pltpu.make_async_copy(tw.at[STEPS, 0:own_vecs, 0:OWN], out.at[:, own_cols], loc_sem.at[9]).wait()
    for owner in range(nedges):

        @pl.when(x != owner)
        def _(owner=owner):
            finals[owner].wait_send()
            remote(
                tw.at[STEPS, 0:own_vecs, 0:OWN], out.at[:, owner * OWN : (owner + 1) * OWN],
                fin_send.at[owner], fin_recv.at[owner], (r, owner),
            ).wait_recv()


def per_device(nrows, nedges, features, edge_src, edge_dst, edge_cell, cell_bias, w_in, w_out, vectors, cheb_coef):
    ids = [a.reshape(IDROWS, LANES) for a in (edge_src, edge_dst, edge_cell)]
    own_vecs = VEC // nedges
    dma = pltpu.SemaphoreType.DMA
    anywhere = pl.BlockSpec(memory_space=pl.ANY)
    result = pl.pallas_call(
        functools.partial(kernel, nrows, nedges),
        out_shape=jax.ShapeDtypeStruct(vectors.shape, BF16),
        in_specs=[anywhere] * 9,
        out_specs=anywhere,
        scratch_shapes=[
            pltpu.VMEM((E_DEV, HID), BF16),
            pltpu.VMEM((2 * ENDS, HID), BF16),
            pltpu.VMEM((3, IDROWS, LANES), jnp.int32),
            pltpu.VMEM((2, IDROWS, LANES), jnp.int32),
            pltpu.VMEM((2, IDROWS, LANES), jnp.int32),
            pltpu.VMEM((3, 2 * HID), BF16),
            pltpu.SMEM((STEPS + 1,), F32),
            pltpu.VMEM((HID, 2 * HID), BF16),
            pltpu.VMEM((HID, HID), BF16),
            pltpu.VMEM((HID, HID), BF16),
            pltpu.VMEM(vectors.shape, F32),
            pltpu.VMEM(vectors.shape, BF16),
            pltpu.VMEM((1, E_DEV + 2 * ENDS), jnp.int32),
            pltpu.VMEM((E_DEV, LANES), F32),
            pltpu.VMEM((PAIRS, SLOTS, 2 * ENDS), BF16),
            pltpu.VMEM((E_DEV, HID), BF16),
            pltpu.VMEM((E_DEV, HID), BF16),
            pltpu.VMEM((PAIRS, SLOTS, HID), BF16),
            pltpu.VMEM((TROWS * NBAND * TILE, TILE), F32),
            pltpu.VMEM((TROWS, (NBAND + 1) * TILE, TILE), BF16),
            pltpu.VMEM((STEPS + 1, VEC, WIDE), BF16),
            pltpu.VMEM((STEPS - 2, VEC, OWN), F32),
            pltpu.VMEM((VEC, OWN), F32),
            dma((10,)),
            dma((2, 2)),
            dma((2, 2)),
            dma((2,)),
            dma((2,)),
            dma((nedges,)),
            dma((nedges,)),
            dma((2,)),
            dma((2, nedges)),
            dma((STEPS, 2, GROUPS)),
            dma((STEPS, 2, GROUPS)),
            dma((nedges,)),
            dma((nedges,)),
        ],
        compiler_params=pltpu.CompilerParams(
            collective_id=0, has_side_effects=True
        ),
        name="filter",
    )(features, *ids, cell_bias, w_in, w_out, vectors, cheb_coef)
    return result.astype(F32)


def solution(mesh):
    nrows, nedges = mesh.shape["rows"], mesh.shape["edges"]
    placed = (
        P(("rows", "edges"), None),
        P(("rows", "edges")),
        P(("rows", "edges")),
        P(("rows", "edges")),
        P(),
        P(),
        P(),
        P("edges", "rows"),
        P(),
    )
    return jax.shard_map(
        functools.partial(per_device, nrows, nedges),
        mesh=mesh,
        in_specs=placed,
        out_specs=P("edges", "rows"),
        check_vma=False,
    )
```

```python
import functools

import jax
import jax.numpy as jnp
from jax import lax
from jax.experimental import pallas as pl
from jax.experimental.pallas import tpu as pltpu
from jax.sharding import PartitionSpec as P

MESH = pl.DeviceIdType.MESH
BF16 = jnp.bfloat16
F32 = jnp.float32

ORB = 16
TILE_ATOMS = 8
BAND = 3
NBAND = 2 * BAND + 1
HID = 256
VEC = 128
STEPS = 4
ATOM_Q = 32
SPILL = 320
E_DEV = 1280
TILE = TILE_ATOMS * ORB
TROWS = ATOM_Q // TILE_ATOMS
OWN = TROWS * TILE
HALO = BAND * TILE
WIDE = OWN + 2 * HALO
LANES = 128
IDROWS = E_DEV // LANES
PAIRS = TROWS // 2
SLOTS_I = 2 * NBAND * TILE_ATOMS
SLOTS = TILE_ATOMS * SLOTS_I
ENDS = 384
PAD = ENDS - SPILL
GROUPS = 4
GROWS = VEC // GROUPS


def kernel(
    nrows, nedges,
    feat, src, dst, cell, bias, w_in, w_out, vec, coef,
    out,
    fown, fends, ids_own, ids_low, ids_high, bias_v, coef_s, win_v, wout_v, wperm, vec_v, vsend,
    slots, cells, onehot_ends, hid, blk, cmat, ht32, ht, tw, tf, res,
    loc_sem, ids_send, ids_recv, feat_send, feat_recv, win_send, win_recv, rim_send, rim_recv,
    halo_send, halo_recv, fin_send, fin_recv,
):
    r = lax.axis_index("rows")
    x = lax.axis_index("edges")
    quarter = r * nedges + x
    ntiles = nrows * nedges * TROWS
    own_vecs = VEC // nedges

    up_x = lax.rem(x + 1, nedges)
    up_r = lax.rem(r + (x + 1) // nedges, nrows)
    down_x = lax.rem(x + nedges - 1, nedges)
    down_r = lax.rem(r + nrows - 1 + (x + nedges - 1) // nedges, nrows)
    up = (up_r, up_x)
    down = (down_r, down_x)

    def remote(source, target, send, recv, device):
        return pltpu.make_async_remote_copy(
            src_ref=source, dst_ref=target, send_sem=send, recv_sem=recv,
            device_id=device, device_id_type=MESH,
        )

    loads = [
        pltpu.make_async_copy(vec, vec_v, loc_sem.at[0]),
        pltpu.make_async_copy(w_out, wout_v, loc_sem.at[1]),
        pltpu.make_async_copy(w_in, win_v, loc_sem.at[2]),
        pltpu.make_async_copy(bias, bias_v, loc_sem.at[3]),
        pltpu.make_async_copy(feat, fown, loc_sem.at[4]),
        pltpu.make_async_copy(src, ids_own.at[0], loc_sem.at[5]),
        pltpu.make_async_copy(dst, ids_own.at[1], loc_sem.at[6]),
        pltpu.make_async_copy(cell, ids_own.at[2], loc_sem.at[7]),
        pltpu.make_async_copy(coef, coef_s, loc_sem.at[8]),
    ]
    barrier = pltpu.get_barrier_semaphore()
    after_r = lax.rem(r + 1, nrows)
    before_r = lax.rem(r + nrows - 1, nrows)

    def greet(device):
        pl.semaphore_signal(barrier, inc=1, device_id=device, device_id_type=MESH)

    for device in [up, down] + [(r, lax.rem(x + off, nedges)) for off in range(1, nedges)]:
        greet(device)

    @pl.when(x == 0)
    def _():
        for n in range(nedges):
            greet((before_r, n))

    @pl.when(x == nedges - 1)
    def _():
        for n in range(nedges):
            greet((after_r, n))

    for load in loads:
        load.start()

    loads[1].wait()
    k_id = lax.broadcasted_iota(jnp.int32, (HID, HID), 0)
    n_id = lax.broadcasted_iota(jnp.int32, (HID, HID), 1)
    swap = jnp.logical_and(n_id // ORB == k_id % ORB, n_id % ORB == k_id // ORB)
    perm = jnp.where(swap, 1.0, 0.0).astype(BF16)
    wperm[...] = jnp.dot(wout_v[...], perm, preferred_element_type=F32).astype(BF16)
    for load in loads[2:]:
        load.wait()
    half = jnp.where(lax.broadcasted_iota(jnp.int32, (1, 2 * HID), 1) < HID, 0.5, 1.0)
    win_v[...] = (win_v[...].astype(F32) * half).astype(BF16)
    bias_of = [bias_v[n : n + 1, :].astype(F32) * half for n in range(3)]

    def pair_net(at, count):
        for n in range(at, at + count, LANES):
            row = ids_own[2, n // LANES : n // LANES + 1, :]
            cells[n : n + LANES, :] = jnp.broadcast_to(row.astype(F32), (LANES, LANES)).T
        for first in range(at, at + count, 128):
            rows = slice(first, first + 128)
            kind = cells[rows, :]
            second, third = kind > 0.5, kind > 1.5
            pre = jnp.dot(fown[rows, :], win_v[...], preferred_element_type=F32)
            parts = []
            for c in range(0, 2 * HID, LANES):
                b0, b1, b2 = [b[:, c : c + LANES] for b in bias_of]
                parts.append(pre[:, c : c + LANES] + jnp.where(third, b2, jnp.where(second, b1, b0)))
            for n in range(HID // LANES):
                gate = parts[n]
                value = (gate + gate * jnp.tanh(gate)) * parts[n + HID // LANES]
                hid[rows, n * LANES : (n + 1) * LANES] = value.astype(BF16)
        rows = slice(at, at + count)
        blk[rows, :] = jnp.dot(hid[rows, :], wperm[...], preferred_element_type=F32).astype(BF16)

    def slot_ids(ids):
        source = ids[0]
        goal = ids[1]
        local = source % ATOM_Q
        shift = goal // TILE_ATOMS - source // TILE_ATOMS + BAND
        shift = jnp.where(shift < 0, shift + ntiles, shift)
        shift = jnp.where(shift >= ntiles, shift - ntiles, shift)
        tile = local // TILE_ATOMS
        slot = (
            tile // 2 * SLOTS
            + (local % TILE_ATOMS) * SLOTS_I
            + (tile % 2 * NBAND + shift) * TILE_ATOMS
            + goal % TILE_ATOMS
        )
        return jnp.where(source // ATOM_Q == quarter, slot, -1)

    ends_rows = (slice(0, ENDS), slice(E_DEV - ENDS, E_DEV))
    for rows in ends_rows:
        pair_net(rows.start, ENDS)

    loads[0].wait()
    vsend[...] = vec_v[...].astype(BF16)
    own_cols = pl.ds(pl.multiple_of(x * OWN, OWN), OWN)
    own_rows = pl.ds(pl.multiple_of(x * own_vecs, own_vecs), own_vecs)
    fends[0:PAD, :] = jnp.zeros((PAD, HID), BF16)
    fends[2 * ENDS - PAD : 2 * ENDS, :] = jnp.zeros((PAD, HID), BF16)

    pl.semaphore_wait(barrier, nedges + 3)

    id_copies = []
    for n, ref in enumerate((src, dst)):
        id_copies.append(remote(ref, ids_low.at[n], ids_send.at[0, n], ids_recv.at[0, n], up))
        id_copies.append(remote(ref, ids_high.at[n], ids_send.at[1, n], ids_recv.at[1, n], down))
    blk_copies = [
        remote(blk.at[E_DEV - SPILL : E_DEV], fends.at[PAD:ENDS], feat_send.at[0], feat_recv.at[0], up),
        remote(blk.at[0:SPILL], fends.at[ENDS : ENDS + SPILL], feat_send.at[1], feat_recv.at[1], down),
    ]
    for copy in id_copies + blk_copies:
        copy.start()
    pair_net(ENDS, E_DEV - 2 * ENDS)

    windows = []
    for n in range(nedges):
        first = max(n * OWN - HALO, 0)
        last = min((n + 1) * OWN + HALO, nedges * OWN)
        at = first - (n * OWN - HALO)
        windows.append((first, last, at))

    def window(n, source):
        first, last, at = windows[n]
        rows = pl.ds(pl.multiple_of(source * own_vecs, own_vecs), own_vecs)
        return remote(
            vsend.at[:, first:last], tw.at[0, rows, at : at + last - first],
            win_send.at[n], win_recv.at[source], (r, n),
        )

    def rim(side, source):
        rows = pl.ds(pl.multiple_of(source * own_vecs, own_vecs), own_vecs)
        if side == 0:
            source_cols, cols, device = slice(nedges * OWN - HALO, nedges * OWN), slice(0, HALO), (after_r, 0)
        else:
            source_cols, cols, device = slice(0, HALO), slice(HALO + OWN, WIDE), (before_r, nedges - 1)
        return remote(
            vsend.at[:, source_cols], tw.at[0, rows, cols],
            rim_send.at[side], rim_recv.at[side, source], device,
        )

    own_slots = slot_ids(ids_own)
    for c in range(IDROWS):
        slots[:, c * LANES : (c + 1) * LANES] = own_slots[c : c + 1, :]

    place = lax.broadcasted_iota(jnp.int32, (SLOTS, 1), 0)

    def place_own(pair):
        row = slots[:, 0:E_DEV] - pair * SLOTS
        onehot = jnp.where(row == place, 1.0, 0.0).astype(BF16)
        own = jnp.dot(onehot, blk[0:E_DEV, :], preferred_element_type=F32)
        cmat[pair] = own.astype(BF16)

    place_own(0)
    own_rims = [rim(side, x) for side in range(2)]
    for copy in own_rims:
        copy.start()
    for n in range(nedges):

        @pl.when(lax.rem(x + 2, nedges) == n)
        def _(n=n):
            window(n, x).start()

    for n in range(nedges):

        @pl.when(jnp.logical_and(x != n, lax.rem(x + 2, nedges) != n))
        def _(n=n):
            window(n, x).start()

    for n in range(nedges):

        @pl.when(x == n)
        def _(n=n):
            first, last, at = windows[n]
            tw[0, own_rows, at : at + last - first] = vsend[:, first:last]

    place_own(1)

    def halo(step, group, rows):
        return [
            remote(
                tw.at[step, rows, HALO + OWN - HALO : HALO + OWN], tw.at[step, rows, 0:HALO],
                halo_send.at[step, 0, group], halo_recv.at[step, 0, group], up,
            ),
            remote(
                tw.at[step, rows, HALO : 2 * HALO], tw.at[step, rows, HALO + OWN : WIDE],
                halo_send.at[step, 1, group], halo_recv.at[step, 1, group], down,
            ),
        ]

    group_rows = [slice(g * GROWS, (g + 1) * GROWS) for g in range(GROUPS)]
    halos = {}

    for copy in id_copies:
        copy.wait_recv()
    low_slots = slot_ids(ids_low)
    high_slots = slot_ids(ids_high)
    nends = ENDS // LANES
    for c in range(nends):
        low_row = slice(IDROWS - nends + c, IDROWS - nends + c + 1)
        high_row = slice(c, c + 1)
        at = E_DEV + c * LANES
        slots[:, at : at + LANES] = low_slots[low_row, :]
        at = at + ENDS
        slots[:, at : at + LANES] = high_slots[high_row, :]

    @pl.loop(0, PAIRS)
    def _(pair):
        row = slots[:, E_DEV : E_DEV + 2 * ENDS] - pair * SLOTS
        onehot_ends[pair] = jnp.where(row == place, 1.0, 0.0).astype(BF16)

    for t in range(TROWS):
        free = 0 if t % 2 else NBAND * TILE
        ht[t, free : free + TILE, :] = jnp.zeros((TILE, TILE), BF16)
    for copy in blk_copies:
        copy.wait_recv()

    group = lax.broadcasted_iota(jnp.int32, (16, LANES), 1)
    odd = [(group & (ORB << bit)) != 0 for bit in range(3)]
    for pair in range(PAIRS):
        ends = jnp.dot(onehot_ends[pair], fends[...], preferred_element_type=F32)
        cmat[pair] = cmat[pair] + ends.astype(BF16)
    for pair in range(PAIRS):
        for k in range(NBAND):
            for side in range(2):
                cols = slice(side * LANES, (side + 1) * LANES)
                parts = []
                for i in range(TILE_ATOMS):
                    at = i * SLOTS_I + 16 * k
                    part = cmat[pair, at : at + 16, cols]
                    parts.append(pltpu.roll(part, i * ORB, 1) if i else part)
                for q in range(8):
                    level = [parts[(g - q) % 8] for g in range(8)]
                    for bit in range(3):
                        level = [
                            jnp.where(odd[bit], level[n + 1], level[n])
                            for n in range(0, len(level), 2)
                        ]
                    both = pltpu.roll(level[0], LANES - q * ORB, 1) if q else level[0]
                    both = both.astype(F32)
                    for s in range(2):
                        start = (pair * 2 * NBAND + 2 * k + s) * TILE + (side * 8 + q) * TILE_ATOMS
                        ht32[start : start + TILE_ATOMS, :] = both[8 * s : 8 * s + 8, :]
            for s in range(2):
                a, d = divmod(2 * k + s, NBAND)
                for j in range(TILE_ATOMS):
                    start = (pair * 2 * NBAND + 2 * k + s) * TILE + j
                    piece = ht32[pl.ds(start, ORB, stride=TILE_ATOMS), :].astype(BF16)
                    at = (a + d) * TILE + j * ORB
                    ht[2 * pair + a, at : at + ORB, :] = piece

    def wait_windows(sources):
        for n in range(nedges):

            @pl.when(x == n)
            def _(n=n):
                for source in sources:
                    if source != n:
                        window(n, source).wait_recv()
                    if n == 0:
                        rim(0, source).wait_recv()
                    if n == nedges - 1:
                        rim(1, source).wait_recv()

    finals = []
    for step in range(1, STEPS + 1):
        for g in range(GROUPS):
            rows = group_rows[g]
            if step == 1:
                wait_windows(range(g * GROWS // own_vecs, (g + 1) * GROWS // own_vecs))
            else:
                for copy in halos[step - 1, g]:
                    copy.wait_recv()
            for pair in range(PAIRS):
                cols = slice(pair * 2 * TILE, (pair + 1) * 2 * TILE)
                wide = slice(pair * 2 * TILE, pair * 2 * TILE + (NBAND + 1) * TILE)
                band = jnp.concatenate([ht[2 * pair], ht[2 * pair + 1]], axis=1)
                product = jnp.dot(tw[step - 1, rows, wide], band, preferred_element_type=F32)
                mid = slice(HALO + pair * 2 * TILE, HALO + (pair + 1) * 2 * TILE)
                if step == 1:
                    new = product
                    total = coef_s[0] * tw[0, rows, mid].astype(F32) + coef_s[1] * new
                else:
                    if step == 2:
                        older = tw[0, rows, mid].astype(F32)
                    else:
                        older = tf[step - 3, rows, cols]
                    new = 2.0 * product - older
                    total = res[rows, cols] + coef_s[step] * new
                if step < STEPS:
                    tw[step, rows, mid] = new.astype(BF16)
                if step < STEPS - 1:
                    tf[step - 1, rows, cols] = new
                if step < STEPS:
                    res[rows, cols] = total
                else:
                    fsend = tw.at[STEPS]
                    fsend[rows, cols] = total.astype(BF16)
            if step < STEPS:
                halos[step, g] = halo(step, g, rows)
                for copy in halos[step, g]:
                    copy.start()
            else:
                for owner in range(g * GROWS // own_vecs, (g + 1) * GROWS // own_vecs):
                    vecs = slice(owner * own_vecs, (owner + 1) * own_vecs)
                    copy = remote(
                        tw.at[STEPS, vecs, 0:OWN], out.at[:, own_cols],
                        fin_send.at[owner], fin_recv.at[x], (r, owner),
                    )
                    finals.append(copy)

                    @pl.when(x != owner)
                    def _(copy=copy):
                        copy.start()

                    @pl.when(x == owner)
                    def _(vecs=vecs):
                        pltpu.make_async_copy(tw.at[STEPS, vecs, 0:OWN], out.at[:, own_cols], loc_sem.at[9]).start()

    for copy in id_copies + blk_copies + own_rims:
        copy.wait_send()
    for n in range(nedges):

        @pl.when(x != n)
        def _(n=n):
            window(n, x).wait_send()
    for pair in halos.values():
        for copy in pair:
            copy.wait_send()
    pltpu.make_async_copy(tw.at[STEPS, 0:own_vecs, 0:OWN], out.at[:, own_cols], loc_sem.at[9]).wait()
    for owner in range(nedges):

        @pl.when(x != owner)
        def _(owner=owner):
            finals[owner].wait_send()
            remote(
                tw.at[STEPS, 0:own_vecs, 0:OWN], out.at[:, owner * OWN : (owner + 1) * OWN],
                fin_send.at[owner], fin_recv.at[owner], (r, owner),
            ).wait_recv()


def per_device(nrows, nedges, features, edge_src, edge_dst, edge_cell, cell_bias, w_in, w_out, vectors, cheb_coef):
    ids = [a.reshape(IDROWS, LANES) for a in (edge_src, edge_dst, edge_cell)]
    own_vecs = VEC // nedges
    dma = pltpu.SemaphoreType.DMA
    anywhere = pl.BlockSpec(memory_space=pl.ANY)
    result = pl.pallas_call(
        functools.partial(kernel, nrows, nedges),
        out_shape=jax.ShapeDtypeStruct(vectors.shape, BF16),
        in_specs=[anywhere] * 9,
        out_specs=anywhere,
        scratch_shapes=[
            pltpu.VMEM((E_DEV, HID), BF16),
            pltpu.VMEM((2 * ENDS, HID), BF16),
            pltpu.VMEM((3, IDROWS, LANES), jnp.int32),
            pltpu.VMEM((2, IDROWS, LANES), jnp.int32),
            pltpu.VMEM((2, IDROWS, LANES), jnp.int32),
            pltpu.VMEM((3, 2 * HID), BF16),
            pltpu.SMEM((STEPS + 1,), F32),
            pltpu.VMEM((HID, 2 * HID), BF16),
            pltpu.VMEM((HID, HID), BF16),
            pltpu.VMEM((HID, HID), BF16),
            pltpu.VMEM(vectors.shape, F32),
            pltpu.VMEM(vectors.shape, BF16),
            pltpu.VMEM((1, E_DEV + 2 * ENDS), jnp.int32),
            pltpu.VMEM((E_DEV, LANES), F32),
            pltpu.VMEM((PAIRS, SLOTS, 2 * ENDS), BF16),
            pltpu.VMEM((E_DEV, HID), BF16),
            pltpu.VMEM((E_DEV, HID), BF16),
            pltpu.VMEM((PAIRS, SLOTS, HID), BF16),
            pltpu.VMEM((TROWS * NBAND * TILE, TILE), F32),
            pltpu.VMEM((TROWS, (NBAND + 1) * TILE, TILE), BF16),
            pltpu.VMEM((STEPS + 1, VEC, WIDE), BF16),
            pltpu.VMEM((STEPS - 2, VEC, OWN), F32),
            pltpu.VMEM((VEC, OWN), F32),
            dma((10,)),
            dma((2, 2)),
            dma((2, 2)),
            dma((2,)),
            dma((2,)),
            dma((nedges,)),
            dma((nedges,)),
            dma((2,)),
            dma((2, nedges)),
            dma((STEPS, 2, GROUPS)),
            dma((STEPS, 2, GROUPS)),
            dma((nedges,)),
            dma((nedges,)),
        ],
        compiler_params=pltpu.CompilerParams(
            collective_id=0, has_side_effects=True
        ),
        name="filter",
    )(features, *ids, cell_bias, w_in, w_out, vectors, cheb_coef)
    return result.astype(F32)


def solution(mesh):
    nrows, nedges = mesh.shape["rows"], mesh.shape["edges"]
    placed = (
        P(("rows", "edges"), None),
        P(("rows", "edges")),
        P(("rows", "edges")),
        P(("rows", "edges")),
        P(),
        P(),
        P(),
        P("edges", "rows"),
        P(),
    )
    return jax.shard_map(
        functools.partial(per_device, nrows, nedges),
        mesh=mesh,
        in_specs=placed,
        out_specs=P("edges", "rows"),
        check_vma=False,
    )
```

```python
import functools

import jax
import jax.numpy as jnp
from jax import lax
from jax.experimental import pallas as pl
from jax.experimental.pallas import tpu as pltpu
from jax.sharding import PartitionSpec as P

MESH = pl.DeviceIdType.MESH
BF16 = jnp.bfloat16
F32 = jnp.float32

ORB = 16
TILE_ATOMS = 8
BAND = 3
NBAND = 2 * BAND + 1
HID = 256
VEC = 128
STEPS = 4
ATOM_Q = 32
SPILL = 320
E_DEV = 1280
TILE = TILE_ATOMS * ORB
TROWS = ATOM_Q // TILE_ATOMS
OWN = TROWS * TILE
HALO = BAND * TILE
WIDE = OWN + 2 * HALO
LANES = 128
IDROWS = E_DEV // LANES
PAIRS = TROWS // 2
SLOTS_I = 2 * NBAND * TILE_ATOMS
SLOTS = TILE_ATOMS * SLOTS_I
ENDS = 384
PAD = ENDS - SPILL
GROUPS = 4
GROWS = VEC // GROUPS


def kernel(
    nrows, nedges,
    feat, src, dst, cell, bias, w_in, w_out, vec, coef,
    out,
    fown, fends, ids_own, ids_low, ids_high, bias_v, coef_s, win_v, wout_v, wperm, vec_v, vsend,
    slots, cells, onehot_ends, hid, blk, cmat, ht32, ht, tw, tf, res,
    loc_sem, ids_send, ids_recv, feat_send, feat_recv, win_send, win_recv, rim_send, rim_recv,
    halo_send, halo_recv, fin_send, fin_recv,
):
    r = lax.axis_index("rows")
    x = lax.axis_index("edges")
    quarter = r * nedges + x
    ntiles = nrows * nedges * TROWS
    own_vecs = VEC // nedges

    up_x = lax.rem(x + 1, nedges)
    up_r = lax.rem(r + (x + 1) // nedges, nrows)
    down_x = lax.rem(x + nedges - 1, nedges)
    down_r = lax.rem(r + nrows - 1 + (x + nedges - 1) // nedges, nrows)
    up = (up_r, up_x)
    down = (down_r, down_x)

    def remote(source, target, send, recv, device):
        return pltpu.make_async_remote_copy(
            src_ref=source, dst_ref=target, send_sem=send, recv_sem=recv,
            device_id=device, device_id_type=MESH,
        )

    loads = [
        pltpu.make_async_copy(vec, vec_v, loc_sem.at[0]),
        pltpu.make_async_copy(w_out, wout_v, loc_sem.at[1]),
        pltpu.make_async_copy(w_in, win_v, loc_sem.at[2]),
        pltpu.make_async_copy(bias, bias_v, loc_sem.at[3]),
        pltpu.make_async_copy(feat, fown, loc_sem.at[4]),
        pltpu.make_async_copy(src, ids_own.at[0], loc_sem.at[5]),
        pltpu.make_async_copy(dst, ids_own.at[1], loc_sem.at[6]),
        pltpu.make_async_copy(cell, ids_own.at[2], loc_sem.at[7]),
        pltpu.make_async_copy(coef, coef_s, loc_sem.at[8]),
    ]
    barrier = pltpu.get_barrier_semaphore()
    after_r = lax.rem(r + 1, nrows)
    before_r = lax.rem(r + nrows - 1, nrows)

    def greet(device):
        pl.semaphore_signal(barrier, inc=1, device_id=device, device_id_type=MESH)

    for device in [up, down] + [(r, lax.rem(x + off, nedges)) for off in range(1, nedges)]:
        greet(device)

    @pl.when(x == 0)
    def _():
        for n in range(nedges):
            greet((before_r, n))

    @pl.when(x == nedges - 1)
    def _():
        for n in range(nedges):
            greet((after_r, n))

    for load in loads:
        load.start()

    loads[1].wait()
    k_id = lax.broadcasted_iota(jnp.int32, (HID, HID), 0)
    n_id = lax.broadcasted_iota(jnp.int32, (HID, HID), 1)
    swap = jnp.logical_and(n_id // ORB == k_id % ORB, n_id % ORB == k_id // ORB)
    perm = jnp.where(swap, 1.0, 0.0).astype(BF16)
    wperm[...] = jnp.dot(wout_v[...], perm, preferred_element_type=F32).astype(BF16)
    for load in loads[2:]:
        load.wait()
    half = jnp.where(lax.broadcasted_iota(jnp.int32, (1, 2 * HID), 1) < HID, 0.5, 1.0)
    win_v[...] = (win_v[...].astype(F32) * half).astype(BF16)
    bias_of = [bias_v[n : n + 1, :].astype(F32) * half for n in range(3)]

    def pair_net(at, count):
        for n in range(at, at + count, LANES):
            row = ids_own[2, n // LANES : n // LANES + 1, :]
            cells[n : n + LANES, :] = jnp.broadcast_to(row.astype(F32), (LANES, LANES)).T
        for first in range(at, at + count, 128):
            rows = slice(first, first + 128)
            kind = cells[rows, :]
            second, third = kind > 0.5, kind > 1.5
            pre = jnp.dot(fown[rows, :], win_v[...], preferred_element_type=F32)
            parts = []
            for c in range(0, 2 * HID, LANES):
                b0, b1, b2 = [b[:, c : c + LANES] for b in bias_of]
                parts.append(pre[:, c : c + LANES] + jnp.where(third, b2, jnp.where(second, b1, b0)))
            for n in range(HID // LANES):
                gate = parts[n]
                value = (gate + gate * jnp.tanh(gate)) * parts[n + HID // LANES]
                hid[rows, n * LANES : (n + 1) * LANES] = value.astype(BF16)
        rows = slice(at, at + count)
        blk[rows, :] = jnp.dot(hid[rows, :], wperm[...], preferred_element_type=F32).astype(BF16)

    def slot_ids(ids):
        source = ids[0]
        goal = ids[1]
        local = source % ATOM_Q
        shift = goal // TILE_ATOMS - source // TILE_ATOMS + BAND
        shift = jnp.where(shift < 0, shift + ntiles, shift)
        shift = jnp.where(shift >= ntiles, shift - ntiles, shift)
        tile = local // TILE_ATOMS
        slot = (
            tile // 2 * SLOTS
            + (local % TILE_ATOMS) * SLOTS_I
            + (tile % 2 * NBAND + shift) * TILE_ATOMS
            + goal % TILE_ATOMS
        )
        return jnp.where(source // ATOM_Q == quarter, slot, -1)

    ends_rows = (slice(0, ENDS), slice(E_DEV - ENDS, E_DEV))
    for rows in ends_rows:
        pair_net(rows.start, ENDS)

    loads[0].wait()
    vsend[...] = vec_v[...].astype(BF16)
    own_cols = pl.ds(pl.multiple_of(x * OWN, OWN), OWN)
    own_rows = pl.ds(pl.multiple_of(x * own_vecs, own_vecs), own_vecs)
    fends[0:PAD, :] = jnp.zeros((PAD, HID), BF16)
    fends[2 * ENDS - PAD : 2 * ENDS, :] = jnp.zeros((PAD, HID), BF16)

    pl.semaphore_wait(barrier, nedges + 3)

    id_copies = []
    for n, ref in enumerate((src, dst)):
        id_copies.append(remote(ref, ids_low.at[n], ids_send.at[0, n], ids_recv.at[0, n], up))
        id_copies.append(remote(ref, ids_high.at[n], ids_send.at[1, n], ids_recv.at[1, n], down))
    blk_copies = [
        remote(blk.at[E_DEV - SPILL : E_DEV], fends.at[PAD:ENDS], feat_send.at[0], feat_recv.at[0], up),
        remote(blk.at[0:SPILL], fends.at[ENDS : ENDS + SPILL], feat_send.at[1], feat_recv.at[1], down),
    ]
    for copy in id_copies + blk_copies:
        copy.start()
    pair_net(ENDS, E_DEV - 2 * ENDS)

    windows = []
    for n in range(nedges):
        first = max(n * OWN - HALO, 0)
        last = min((n + 1) * OWN + HALO, nedges * OWN)
        at = first - (n * OWN - HALO)
        windows.append((first, last, at))

    def window(n, source):
        first, last, at = windows[n]
        rows = pl.ds(pl.multiple_of(source * own_vecs, own_vecs), own_vecs)
        return remote(
            vsend.at[:, first:last], tw.at[0, rows, at : at + last - first],
            win_send.at[n], win_recv.at[source], (r, n),
        )

    def rim(side, source):
        rows = pl.ds(pl.multiple_of(source * own_vecs, own_vecs), own_vecs)
        if side == 0:
            source_cols, cols, device = slice(nedges * OWN - HALO, nedges * OWN), slice(0, HALO), (after_r, 0)
        else:
            source_cols, cols, device = slice(0, HALO), slice(HALO + OWN, WIDE), (before_r, nedges - 1)
        return remote(
            vsend.at[:, source_cols], tw.at[0, rows, cols],
            rim_send.at[side], rim_recv.at[side, source], device,
        )

    own_slots = slot_ids(ids_own)
    for c in range(IDROWS):
        slots[:, c * LANES : (c + 1) * LANES] = own_slots[c : c + 1, :]

    place = lax.broadcasted_iota(jnp.int32, (SLOTS, 1), 0)

    def place_own(pair):
        row = slots[:, 0:E_DEV] - pair * SLOTS
        onehot = jnp.where(row == place, 1.0, 0.0).astype(BF16)
        own = jnp.dot(onehot, blk[0:E_DEV, :], preferred_element_type=F32)
        cmat[pair] = own.astype(BF16)

    place_own(0)
    for n in range(nedges):

        @pl.when(x != n)
        def _(n=n):
            window(n, x).start()

        @pl.when(x == n)
        def _(n=n):
            first, last, at = windows[n]
            tw[0, own_rows, at : at + last - first] = vsend[:, first:last]

    own_rims = [rim(side, x) for side in range(2)]
    for copy in own_rims:
        copy.start()

    place_own(1)

    def halo(step, group, rows):
        return [
            remote(
                tw.at[step, rows, HALO + OWN - HALO : HALO + OWN], tw.at[step, rows, 0:HALO],
                halo_send.at[step, 0, group], halo_recv.at[step, 0, group], up,
            ),
            remote(
                tw.at[step, rows, HALO : 2 * HALO], tw.at[step, rows, HALO + OWN : WIDE],
                halo_send.at[step, 1, group], halo_recv.at[step, 1, group], down,
            ),
        ]

    group_rows = [slice(g * GROWS, (g + 1) * GROWS) for g in range(GROUPS)]
    halos = {}

    for copy in id_copies:
        copy.wait_recv()
    low_slots = slot_ids(ids_low)
    high_slots = slot_ids(ids_high)
    nends = ENDS // LANES
    for c in range(nends):
        low_row = slice(IDROWS - nends + c, IDROWS - nends + c + 1)
        high_row = slice(c, c + 1)
        at = E_DEV + c * LANES
        slots[:, at : at + LANES] = low_slots[low_row, :]
        at = at + ENDS
        slots[:, at : at + LANES] = high_slots[high_row, :]

    @pl.loop(0, PAIRS)
    def _(pair):
        row = slots[:, E_DEV : E_DEV + 2 * ENDS] - pair * SLOTS
        onehot_ends[pair] = jnp.where(row == place, 1.0, 0.0).astype(BF16)

    for t in range(TROWS):
        free = 0 if t % 2 else NBAND * TILE
        ht[t, free : free + TILE, :] = jnp.zeros((TILE, TILE), BF16)
    for copy in blk_copies:
        copy.wait_recv()

    group = lax.broadcasted_iota(jnp.int32, (16, LANES), 1)
    odd = [(group & (ORB << bit)) != 0 for bit in range(3)]
    for pair in range(PAIRS):
        ends = jnp.dot(onehot_ends[pair], fends[...], preferred_element_type=F32)
        cmat[pair] = cmat[pair] + ends.astype(BF16)
    for pair in range(PAIRS):
        for k in range(NBAND):
            for side in range(2):
                cols = slice(side * LANES, (side + 1) * LANES)
                parts = []
                for i in range(TILE_ATOMS):
                    at = i * SLOTS_I + 16 * k
                    part = cmat[pair, at : at + 16, cols]
                    parts.append(pltpu.roll(part, i * ORB, 1) if i else part)
                for q in range(8):
                    level = [parts[(g - q) % 8] for g in range(8)]
                    for bit in range(3):
                        level = [
                            jnp.where(odd[bit], level[n + 1], level[n])
                            for n in range(0, len(level), 2)
                        ]
                    both = pltpu.roll(level[0], LANES - q * ORB, 1) if q else level[0]
                    both = both.astype(F32)
                    for s in range(2):
                        start = (pair * 2 * NBAND + 2 * k + s) * TILE + (side * 8 + q) * TILE_ATOMS
                        ht32[start : start + TILE_ATOMS, :] = both[8 * s : 8 * s + 8, :]
            for s in range(2):
                a, d = divmod(2 * k + s, NBAND)
                for j in range(TILE_ATOMS):
                    start = (pair * 2 * NBAND + 2 * k + s) * TILE + j
                    piece = ht32[pl.ds(start, ORB, stride=TILE_ATOMS), :].astype(BF16)
                    at = (a + d) * TILE + j * ORB
                    ht[2 * pair + a, at : at + ORB, :] = piece

    def wait_windows(sources):
        for n in range(nedges):

            @pl.when(x == n)
            def _(n=n):
                for source in sources:
                    if source != n:
                        window(n, source).wait_recv()
                    if n == 0:
                        rim(0, source).wait_recv()
                    if n == nedges - 1:
                        rim(1, source).wait_recv()

    def drain():
        for copy in id_copies + blk_copies + own_rims:
            copy.wait_send()
        for n in range(nedges):

            @pl.when(x != n)
            def _(n=n):
                window(n, x).wait_send()

        for step in range(1, STEPS - 1):
            for g in range(GROUPS):
                for copy in halos[step, g]:
                    copy.wait_send()

    finals = []
    for step in range(1, STEPS + 1):
        if step == STEPS:
            drain()
        for g in range(GROUPS):
            rows = group_rows[g]
            if step == 1:
                wait_windows(range(g * GROWS // own_vecs, (g + 1) * GROWS // own_vecs))
            else:
                for copy in halos[step - 1, g]:
                    copy.wait_recv()
            for pair in range(PAIRS):
                cols = slice(pair * 2 * TILE, (pair + 1) * 2 * TILE)
                wide = slice(pair * 2 * TILE, pair * 2 * TILE + (NBAND + 1) * TILE)
                band = jnp.concatenate([ht[2 * pair], ht[2 * pair + 1]], axis=1)
                product = jnp.dot(tw[step - 1, rows, wide], band, preferred_element_type=F32)
                mid = slice(HALO + pair * 2 * TILE, HALO + (pair + 1) * 2 * TILE)
                if step == 1:
                    new = product
                    total = coef_s[0] * tw[0, rows, mid].astype(F32) + coef_s[1] * new
                else:
                    if step == 2:
                        older = tw[0, rows, mid].astype(F32)
                    else:
                        older = tf[step - 3, rows, cols]
                    new = 2.0 * product - older
                    total = res[rows, cols] + coef_s[step] * new
                if step < STEPS:
                    tw[step, rows, mid] = new.astype(BF16)
                if step < STEPS - 1:
                    tf[step - 1, rows, cols] = new
                if step < STEPS:
                    res[rows, cols] = total
                else:
                    fsend = tw.at[STEPS]
                    fsend[rows, cols] = total.astype(BF16)
            if step < STEPS:
                halos[step, g] = halo(step, g, rows)
                for copy in halos[step, g]:
                    copy.start()
            else:
                for owner in range(g * GROWS // own_vecs, (g + 1) * GROWS // own_vecs):
                    vecs = slice(owner * own_vecs, (owner + 1) * own_vecs)
                    copy = remote(
                        tw.at[STEPS, vecs, 0:OWN], out.at[:, own_cols],
                        fin_send.at[owner], fin_recv.at[x], (r, owner),
                    )
                    finals.append(copy)

                    @pl.when(x != owner)
                    def _(copy=copy):
                        copy.start()

                    @pl.when(x == owner)
                    def _(vecs=vecs):
                        pltpu.make_async_copy(tw.at[STEPS, vecs, 0:OWN], out.at[:, own_cols], loc_sem.at[9]).start()

    for g in range(GROUPS):
        for copy in halos[STEPS - 1, g]:
            copy.wait_send()
    pltpu.make_async_copy(tw.at[STEPS, 0:own_vecs, 0:OWN], out.at[:, own_cols], loc_sem.at[9]).wait()
    for owner in range(nedges):

        @pl.when(x != owner)
        def _(owner=owner):
            finals[owner].wait_send()
            remote(
                tw.at[STEPS, 0:own_vecs, 0:OWN], out.at[:, owner * OWN : (owner + 1) * OWN],
                fin_send.at[owner], fin_recv.at[owner], (r, owner),
            ).wait_recv()


def per_device(nrows, nedges, features, edge_src, edge_dst, edge_cell, cell_bias, w_in, w_out, vectors, cheb_coef):
    ids = [a.reshape(IDROWS, LANES) for a in (edge_src, edge_dst, edge_cell)]
    own_vecs = VEC // nedges
    dma = pltpu.SemaphoreType.DMA
    anywhere = pl.BlockSpec(memory_space=pl.ANY)
    result = pl.pallas_call(
        functools.partial(kernel, nrows, nedges),
        out_shape=jax.ShapeDtypeStruct(vectors.shape, BF16),
        in_specs=[anywhere] * 9,
        out_specs=anywhere,
        scratch_shapes=[
            pltpu.VMEM((E_DEV, HID), BF16),
            pltpu.VMEM((2 * ENDS, HID), BF16),
            pltpu.VMEM((3, IDROWS, LANES), jnp.int32),
            pltpu.VMEM((2, IDROWS, LANES), jnp.int32),
            pltpu.VMEM((2, IDROWS, LANES), jnp.int32),
            pltpu.VMEM((3, 2 * HID), BF16),
            pltpu.SMEM((STEPS + 1,), F32),
            pltpu.VMEM((HID, 2 * HID), BF16),
            pltpu.VMEM((HID, HID), BF16),
            pltpu.VMEM((HID, HID), BF16),
            pltpu.VMEM(vectors.shape, F32),
            pltpu.VMEM(vectors.shape, BF16),
            pltpu.VMEM((1, E_DEV + 2 * ENDS), jnp.int32),
            pltpu.VMEM((E_DEV, LANES), F32),
            pltpu.VMEM((PAIRS, SLOTS, 2 * ENDS), BF16),
            pltpu.VMEM((E_DEV, HID), BF16),
            pltpu.VMEM((E_DEV, HID), BF16),
            pltpu.VMEM((PAIRS, SLOTS, HID), BF16),
            pltpu.VMEM((TROWS * NBAND * TILE, TILE), F32),
            pltpu.VMEM((TROWS, (NBAND + 1) * TILE, TILE), BF16),
            pltpu.VMEM((STEPS + 1, VEC, WIDE), BF16),
            pltpu.VMEM((STEPS - 2, VEC, OWN), F32),
            pltpu.VMEM((VEC, OWN), F32),
            dma((10,)),
            dma((2, 2)),
            dma((2, 2)),
            dma((2,)),
            dma((2,)),
            dma((nedges,)),
            dma((nedges,)),
            dma((2,)),
            dma((2, nedges)),
            dma((STEPS, 2, GROUPS)),
            dma((STEPS, 2, GROUPS)),
            dma((nedges,)),
            dma((nedges,)),
        ],
        compiler_params=pltpu.CompilerParams(
            collective_id=0, has_side_effects=True
        ),
        name="filter",
    )(features, *ids, cell_bias, w_in, w_out, vectors, cheb_coef)
    return result.astype(F32)


def solution(mesh):
    nrows, nedges = mesh.shape["rows"], mesh.shape["edges"]
    placed = (
        P(("rows", "edges"), None),
        P(("rows", "edges")),
        P(("rows", "edges")),
        P(("rows", "edges")),
        P(),
        P(),
        P(),
        P("edges", "rows"),
        P(),
    )
    return jax.shard_map(
        functools.partial(per_device, nrows, nedges),
        mesh=mesh,
        in_specs=placed,
        out_specs=P("edges", "rows"),
        check_vma=False,
    )
```
